32 devices in a mesh: clusters: 32 (over z, y, x, core).
Axes of the slice: x: 2, y: 2, z: 4, core: 2. Of those that a mesh axis runs over, the one named last changes fastest.
Arguments:
- charges: bfloat16 [8, 131072], P(None, 'clusters'), may hold values from -6 to 6
- leaf_basis: bfloat16 [32, 131072], P(None, 'clusters'), may hold values from -0.75 to 0.75
- leaf_transfer: bfloat16 [256, 64, 256], P('clusters'), may hold values from -0.375 to 0.375
- mid_transfer: bfloat16 [32, 64, 512], P('clusters'), may hold values from -0.25 to 0.25
- far_source: int32 [2048, 16], P('clusters'), may hold values from 0 to 2047, as said below
- far_coupling: bfloat16 [2048, 32, 512], P('clusters'), may hold values from -0.25 to 0.25
- mid_source: int32 [256, 8], P('clusters'), may hold values from 0 to 255, as said below
- mid_coupling: bfloat16 [256, 64, 512], P('clusters'), may hold values from -0.25 to 0.25
- box_coupling: bfloat16 [32, 64, 192], P('clusters'), may hold values from -0.4375 to 0.4375
- top_transfer: bfloat16 [28, 64, 128], replicated, may hold values from -0.5 to 0.5
- top_coupling: bfloat16 [28, 64, 192], replicated, may hold values from -0.4375 to 0.4375
- near_target: int32 [32768], P('clusters'), may hold values from 0 to 63
- near_source: int32 [32768], P('clusters'), may hold values from 0 to 2047, as said below
- near_count: int32 [32], P('clusters'), may hold values from 256 to 1024, as said below
- near_blocks: bfloat16 [64, 2097152], P(None, 'clusters'), may hold values from -0.25 to 0.25
Outputs:
- potentials: bfloat16 [8, 131072], P(None, 'clusters')
The draws below stay inside these ranges and needn't reach their ends.
Inputs may be any that keep to these rules, and one draw needn't show every extreme that they name: `far_source`: each source leaf lies in the row's box or in a box whose index differs by one; for each box and each box beside it, the far lists of the box's leaves name exactly 4 distinct leaves of the box beside it. `mid_source`: each source cluster lies in the row's box or in a box whose index differs by one. `near_source`: each source leaf lies in the slot's box or in a box whose index differs by one. `near_count`: slots at or after a box's count are not used.
All inputs are finite; a program needn't handle non-finite values.
Results may differ from the reference program's by a relative error of at most 0.0053.
Values may be sent and summed in bfloat16 or wider, within the bound.
A program may use at most 128 MiB of HBM per device.

```python
import jax
import jax.numpy as jnp
from jax import lax

M = 64
NV = 8
R0 = 32
R = 64
CHILD = 8
K0 = 16
K1 = 8
SLOT = 4
NB_CAP = 1024
BOXES = 32
LEAF_DEV = 64
NL = 2048
NL1 = 256
POINTS = 131072
NBALL = 32768
LEVELS_TOP = 3
TOPS = 28


def shuffled(subkey, length):
    return jax.random.permutation(subkey, length).astype(jnp.int32)


def draw_far_source(key, part):
    devices = NL // LEAF_DEV
    entries = LEAF_DEV * K0
    kinds = 2 * SLOT
    key_sets, key_extra, key_mix = jax.random.split(jax.random.fold_in(key, 11), 3)
    scores = jax.random.randint(key_sets, (devices, 2, LEAF_DEV), 0, 1 << 20) * LEAF_DEV + jnp.arange(LEAF_DEV, dtype=jnp.int32)
    chosen = jnp.argsort(scores, axis=-1, stable=True)[:, :, :SLOT].astype(jnp.int32)
    forced = jnp.broadcast_to(jnp.arange(kinds, dtype=jnp.int32)[None, :], (devices, kinds))
    extra = jax.random.randint(key_extra, (devices, entries - kinds), 0, 2 * kinds + LEAF_DEV).astype(jnp.int32)
    pooled = jnp.concatenate([forced, extra], axis=1)
    mixing = jax.vmap(lambda subkey: shuffled(subkey, entries))(jax.random.split(key_mix, devices))
    pooled = jnp.take_along_axis(pooled, mixing, axis=1)
    rows = jnp.arange(devices, dtype=jnp.int32)[:, None]
    is_side = pooled < 2 * kinds
    code = pooled % kinds
    side = code // SLOT
    within = code % SLOT
    picked = chosen[rows, side, within]
    neighbour = rows + 2 * side - 1
    valid = is_side & (neighbour >= 0) & (neighbour < devices)
    own_leaf = jnp.where(is_side, picked, pooled - 2 * kinds)
    leaf = jnp.where(valid, neighbour * LEAF_DEV + picked, rows * LEAF_DEV + own_leaf)
    return leaf.reshape(NL, K0).astype(jnp.int32)


def draw_mid_source(key, part):
    devices = NL1 // CHILD
    key_step, key_box, key_mix = jax.random.split(key, 3)
    home = jnp.arange(NL1, dtype=jnp.int32)[:, None] // CHILD
    moves = jax.random.randint(key_step, (NL1, K1), -1, 2).astype(jnp.int32)
    column = jnp.arange(K1, dtype=jnp.int32)[None, :]
    moves = jnp.where(column == 0, -1, jnp.where(column == 1, 1, moves))
    mixing = jax.vmap(lambda subkey: shuffled(subkey, K1))(jax.random.split(key_mix, NL1))
    moves = jnp.take_along_axis(moves, mixing, axis=1)
    target = home + moves
    target = jnp.where(target < 0, home + 1, jnp.where(target >= devices, home - 1, target))
    inside = jax.random.randint(key_box, (NL1, K1), 0, CHILD).astype(jnp.int32)
    return (target * CHILD + inside).astype(jnp.int32)


def draw_near_source(key, part):
    devices = NBALL // NB_CAP
    key_step, key_leaf, key_place = jax.random.split(key, 3)
    home = jnp.arange(NBALL, dtype=jnp.int32) // NB_CAP
    position = jnp.arange(NBALL, dtype=jnp.int32) % NB_CAP
    anchor = jax.random.randint(key_place, (devices,), 0, max(NB_CAP // 4 - 1, 1)).astype(jnp.int32)[home]
    moves = jax.random.randint(key_step, (NBALL,), -1, 2).astype(jnp.int32)
    moves = jnp.where(position == anchor, -1, jnp.where(position == anchor + 1, 1, moves))
    target = home + moves
    target = jnp.where(target < 0, home + 1, jnp.where(target >= devices, home - 1, target))
    inside = jax.random.randint(key_leaf, (NBALL,), 0, LEAF_DEV).astype(jnp.int32)
    return (target * LEAF_DEV + inside).astype(jnp.int32)


def draw_near_count(key, part):
    devices = NBALL // NB_CAP
    key_base, key_top = jax.random.split(key)
    base = jax.random.randint(key_base, (devices,), NB_CAP // 4, NB_CAP // 2 + 1).astype(jnp.int32)
    fullest = jax.random.randint(key_top, (), 0, devices).astype(jnp.int32)
    index = jnp.arange(devices, dtype=jnp.int32)
    full = (index == fullest) | (index == devices - 1)
    return jnp.where(full, NB_CAP, base).astype(jnp.int32)


def place_ends(result, key, low, top_value):
    shape = result.shape
    place = [jax.random.randint(jax.random.fold_in(key, axis), (), 0, shape[axis]) for axis in range(len(shape))]
    result = result.at[tuple(place)].set(low)
    longest = shape.index(max(shape))
    place[longest] = (place[longest] + 1) % shape[longest]
    return result.at[tuple(place)].set(top_value)


def steps_of(rng, dims, cuts, smallest, top_value):
    def one(axis_at, blocks):
        heights = jax.random.uniform(jax.random.fold_in(jax.random.fold_in(rng, 6), axis_at), (blocks,), jnp.float32, smallest / len(cuts), top_value / len(cuts))
        return jnp.repeat(jnp.exp(heights), dims[axis_at] // blocks).reshape((-1,) + (1,) * (len(dims) - axis_at - 1))

    level = one(*cuts[0])
    for cut in cuts[1:]:
        level = level * one(*cut)
    return level


def normal_values(key, shape, width, bound, pieces=(), kind=jnp.bfloat16):
    result = jax.random.normal(key, shape, jnp.float32) * width
    if len(pieces) > 0:
        result = steps_of(key, shape, pieces, -0.22, 0.18) * result
    return jnp.clip(result, min=-bound, max=bound).astype(kind)


def setup_inputs(seed: int = 0) -> dict:
    key_list = jax.random.split(jax.random.key(seed), 16)
    charges = normal_values(key_list[0], (NV, POINTS), 1.0, 6.0, ((1, 32),))
    leaf_basis = normal_values(key_list[1], (R0, POINTS), M ** -0.5, 0.75, ((1, 32),))
    leaf_transfer = normal_values(key_list[2], (NL1, R, CHILD * R0), (CHILD * R0) ** -0.5, 0.375, ((0, 32),))
    mid_transfer = normal_values(key_list[3], (BOXES, R, CHILD * R), (CHILD * R) ** -0.5, 0.25, ((0, 32),))
    far_source = draw_far_source(jax.random.fold_in(key_list[15], 71), 0)
    far_coupling = normal_values(key_list[5], (NL, R0, K0 * R0), (K0 * R0) ** -0.5, 0.25, ((0, 32),))
    mid_source = draw_mid_source(jax.random.fold_in(key_list[15], 71), 0)
    mid_coupling = normal_values(key_list[7], (NL1, R, K1 * R), (K1 * R) ** -0.5, 0.25, ((0, 32),))
    box_coupling = normal_values(key_list[8], (BOXES, R, 3 * R), (3 * R) ** -0.5, 0.4375, ((0, 32),))
    top_transfer = normal_values(key_list[9], (TOPS, R, 2 * R), (2 * R) ** -0.5, 0.5)
    top_coupling = normal_values(key_list[10], (TOPS, R, 3 * R), (3 * R) ** -0.5, 0.4375)
    near_target = place_ends(jax.random.randint(key_list[11], (NBALL,), 0, LEAF_DEV), jax.random.fold_in(key_list[11], 1), 0, LEAF_DEV - 1).astype(jnp.int32)
    near_source = draw_near_source(jax.random.fold_in(key_list[15], 71), 0)
    near_count = draw_near_count(jax.random.fold_in(key_list[15], 71), 0)
    near_blocks = normal_values(key_list[14], (M, NBALL * M), (8 * M) ** -0.5, 0.25, ((1, 32),))
    return dict(charges=charges, leaf_basis=leaf_basis, leaf_transfer=leaf_transfer, mid_transfer=mid_transfer, far_source=far_source, far_coupling=far_coupling, mid_source=mid_source, mid_coupling=mid_coupling, box_coupling=box_coupling, top_transfer=top_transfer, top_coupling=top_coupling, near_target=near_target, near_source=near_source, near_count=near_count, near_blocks=near_blocks)


deepest_level = lax.Precision.HIGHEST


def level_partners(upward):
    count = upward.shape[0]
    padded = jnp.pad(upward, ((3, 3), (0, 0), (0, 0)))
    is_even = (jnp.arange(count) % 2 == 0)[:, None, None]
    back_three = padded[0:count]
    back_two = padded[1:count + 1]
    ahead_two = padded[5:count + 5]
    ahead_three = padded[6:count + 6]
    return jnp.concatenate([jnp.where(is_even, back_two, back_three), jnp.where(is_even, ahead_two, back_two), jnp.where(is_even, ahead_three, ahead_two)], axis=1)


def reference(charges, leaf_basis, leaf_transfer, mid_transfer, far_source, far_coupling, mid_source, mid_coupling, box_coupling, top_transfer, top_coupling, near_target, near_source, near_count, near_blocks):
    leaves = NL
    groups = NL1
    charge_cube = charges.reshape(NV, leaves, M).astype(jnp.float32)
    basis_tensor = leaf_basis.reshape(R0, leaves, M).astype(jnp.float32)
    leaf_up = jnp.einsum('rlm,vlm->lrv', basis_tensor, charge_cube, precision=deepest_level).astype(jnp.bfloat16)
    mid_up = jnp.einsum('crk,ckv->crv', leaf_transfer.astype(jnp.float32), leaf_up.reshape(groups, CHILD * R0, NV).astype(jnp.float32), precision=deepest_level).astype(jnp.bfloat16)
    box_up = jnp.einsum('drk,dkv->drv', mid_transfer.astype(jnp.float32), mid_up.reshape(BOXES, CHILD * R, NV).astype(jnp.float32), precision=deepest_level)
    upward = [box_up]
    for level in range(LEVELS_TOP):
        count = BOXES >> (level + 1)
        start = BOXES - (BOXES >> level)
        parents = top_transfer[start:start + count].astype(jnp.float32)
        upward.append(jnp.einsum('prk,pkv->prv', parents, upward[-1].reshape(count, 2 * R, NV), precision=deepest_level))
    across = []
    for level in range(LEVELS_TOP + 1):
        count = BOXES >> level
        if level == 0:
            matrix_stack = box_coupling
        else:
            start = BOXES - (BOXES >> (level - 1))
            matrix_stack = top_coupling[start:start + count]
        across.append(jnp.einsum('crk,ckv->crv', matrix_stack.astype(jnp.float32), level_partners(upward[level]), precision=deepest_level))
    downward = across[LEVELS_TOP]
    for level in range(LEVELS_TOP - 1, -1, -1):
        count = BOXES >> (level + 1)
        start = BOXES - (BOXES >> level)
        parents = top_transfer[start:start + count].astype(jnp.float32)
        pushed = jnp.einsum('prk,prv->pkv', parents, downward, precision=deepest_level).reshape(2 * count, R, NV)
        downward = across[level] + pushed
    box_down = downward.astype(jnp.bfloat16)
    mid_picked = mid_up[mid_source].reshape(groups, K1 * R, NV).astype(jnp.float32)
    mid_far = jnp.einsum('crk,ckv->crv', mid_coupling.astype(jnp.float32), mid_picked, precision=deepest_level)
    mid_push = jnp.einsum('drk,drv->dkv', mid_transfer.astype(jnp.float32), box_down.astype(jnp.float32), precision=deepest_level).reshape(groups, R, NV)
    mid_down = (mid_far + mid_push).astype(jnp.bfloat16)
    leaf_picked = leaf_up[far_source].reshape(leaves, K0 * R0, NV).astype(jnp.float32)
    leaf_far = jnp.einsum('lrk,lkv->lrv', far_coupling.astype(jnp.float32), leaf_picked, precision=deepest_level)
    leaf_push = jnp.einsum('crk,crv->ckv', leaf_transfer.astype(jnp.float32), mid_down.astype(jnp.float32), precision=deepest_level).reshape(leaves, R0, NV)
    leaf_down = (leaf_far + leaf_push).astype(jnp.bfloat16)
    far_field = jnp.einsum('rlm,lrv->vlm', basis_tensor, leaf_down.astype(jnp.float32), precision=deepest_level)
    block = min(1024, NBALL)
    owners = jnp.arange(NBALL, dtype=jnp.int32) // NB_CAP
    alive = (jnp.arange(NBALL, dtype=jnp.int32) % NB_CAP) < near_count[owners]
    targets = (owners * LEAF_DEV + near_target).astype(jnp.int32)

    def near_step(step, total):
        first = (step * block).astype(jnp.int32)
        sources = lax.dynamic_slice_in_dim(near_source, first, block)
        dests = lax.dynamic_slice_in_dim(targets, first, block)
        weights = lax.dynamic_slice_in_dim(alive, first, block).astype(jnp.float32)
        dense = lax.dynamic_slice_in_dim(near_blocks, (first * M).astype(jnp.int32), block * M, 1).reshape(M, block, M).astype(jnp.float32)
        gathered = jnp.take(charge_cube, sources, axis=1)
        contribution = jnp.einsum('tbs,vbs->vbt', dense, gathered, precision=deepest_level) * weights[None, :, None]
        return total.at[:, dests, :].add(contribution)

    near_field = lax.fori_loop(0, NBALL // block, near_step, jnp.zeros((NV, leaves, M), jnp.float32))
    return (far_field + near_field).astype(jnp.bfloat16).reshape(NV, POINTS)
```

```python
import functools

import jax
import jax.numpy as jnp
from jax import lax
from jax.experimental import pallas as pl
from jax.experimental.pallas import tpu as pltpu
from jax.sharding import PartitionSpec as P

F32 = jnp.float32
BF16 = jnp.bfloat16
AXIS = "clusters"
NT = (((1,), (1,)), ((), ()))
NN = (((1,), (0,)), ((), ()))
LANES = 128
CHUNKS = 8


def dot_nt(a, b):
    return lax.dot_general(a, b, NT, preferred_element_type=F32)


def dot_nn(a, b):
    return lax.dot_general(a, b, NN, preferred_element_type=F32)


def lanes(shape):
    return lax.broadcasted_iota(jnp.int32, shape, len(shape) - 1)


def rows(shape):
    return lax.broadcasted_iota(jnp.int32, shape, len(shape) - 2)


def diagonal(out, v, width):
    blocks = out.shape[0] // v
    lane = lanes((v, out.shape[1])) // width
    total = jnp.zeros((v, out.shape[1]), F32)
    for block in range(blocks):
        total = jnp.where(lane == block, out[block * v:(block + 1) * v], total)
    return total


def kernel(
    n, sizes,
    near_source_h, far_source_h, mid_source_h, near_count_h, near_target_h,
    charges_h, basis_h, leaf_transfer_h, mid_transfer_h, far_coupling_h, mid_coupling_h,
    box_coupling_h, top_transfer_h, top_coupling_h, near_blocks_h,
    out_ref,
    cw, lw, mw, gathered, basis, leaf_transfer, mid_transfer, far_coupling, mid_coupling,
    box_coupling, top_transfer, top_coupling, near_blocks,
    near_raw, far_raw, mid_raw, near_target, near_source, far_source, mid_source, near_count,
    charge_tiles, leaf_tiles, mid_tiles, contribution, near_part, near_rows, leaf_far, mid_far, weights, response, base,
    assigned,
    load_sem, near_sem, top_sem, index_sem, halo_send, halo_recv, all_send, all_recv, inside_sem,
):
    v, leaves, m, r0, groups, r, k0, k1, capacity = sizes
    child = leaves // groups
    levels = (n // 4).bit_length() - 1
    bits = n.bit_length() - 1
    me = lax.axis_index(AXIS)
    half = lanes((v, LANES)) < m
    low_lane = lanes((v, LANES)) < r

    barrier = pltpu.get_barrier_semaphore()

    pairs = [
        (charges_h, cw.at[1]), (basis_h, basis), (leaf_transfer_h, leaf_transfer), (mid_transfer_h.at[0], mid_transfer),
        (mid_coupling_h, mid_coupling), (far_coupling_h, far_coupling), (box_coupling_h.at[0], box_coupling),
        (top_transfer_h, top_transfer), (near_source_h, near_raw), (far_source_h, far_raw), (mid_source_h, mid_raw),
        (near_target_h, near_target), (near_count_h, near_count),
    ]
    loads = [pltpu.make_async_copy(s, d, load_sem.at[i]) for i, (s, d) in enumerate(pairs)]
    side = capacity // 2
    width = side * m // CHUNKS

    def near_load(chunk, part):
        span = pl.ds(part * side * m + chunk * width, width)
        return pltpu.make_async_copy(
            near_blocks_h.at[:, span], near_blocks.at[:, span], near_sem.at[2 * chunk + part])

    tops = []
    for level in range(1, levels + 1):
        start = n - (n >> (level - 1))
        tops.append(pltpu.make_async_copy(
            top_coupling_h.at[start + (me >> level)], top_coupling.at[level - 1], top_sem.at[level - 1]))

    for i in (0, 1, 2, 3, 8, 9, 10, 11, 12, 6, 7):
        loads[i].start()
    for copy in tops:
        copy.start()
    loads[5].start()
    for chunk in range(CHUNKS):
        near_load(chunk, 0).start()
        near_load(chunk, 1).start()
    loads[4].start()

    def partner(bit):
        return me + (1 << bit) * (1 - 2 * lax.rem(me // (1 << bit), 2))

    beside = me - 1 + 2 * lax.rem(me, 2)
    has_beside = (beside >= 0) & (beside < n)

    for bit in range(bits):
        pl.semaphore_signal(barrier, inc=1, device_id=(partner(bit),), device_id_type=pl.DeviceIdType.MESH)

    @pl.when(has_beside)
    def _():
        pl.semaphore_signal(barrier, inc=1, device_id=(beside,), device_id_type=pl.DeviceIdType.MESH)

    def tell(bit):
        pl.semaphore_signal(
            inside_sem.at[bit], inc=1, device_id=(partner(bit),), device_id_type=pl.DeviceIdType.MESH)

    def told(bit):
        pl.semaphore_wait(inside_sem.at[bit], 1)

    loads[0].wait()
    loads[1].wait()
    span_points = child * m
    lane_leaf = lanes((v, span_points)) // m
    ups = []
    for c in range(groups):
        x = cw[1, :, c * span_points:(c + 1) * span_points].astype(F32)
        lhs = jnp.concatenate([jnp.where(lane_leaf == l, x, 0.0) for l in range(child)], axis=0).astype(BF16)
        b = basis[:, c * span_points:(c + 1) * span_points]
        up = diagonal(dot_nt(lhs, jnp.concatenate([b] * child, axis=0)), v, r0).astype(BF16)
        lw[1, :, c * child * r0:(c + 1) * child * r0] = up
        ups.append(up.astype(F32))
    loads[2].wait()
    loads[3].wait()
    quad = 4
    for g in range(groups // quad):
        lhs = jnp.concatenate(ups[g * quad:(g + 1) * quad], axis=0).astype(BF16)
        matrix = leaf_transfer[g * quad:(g + 1) * quad].reshape(quad * r, child * r0)
        mw[1, :, g * quad * r:(g + 1) * quad * r] = diagonal(dot_nt(lhs, matrix), v, r).astype(BF16)
    transfer = mid_transfer[...]
    box_up = dot_nt(mw[1], jnp.concatenate([transfer, transfer], axis=0))
    gathered[me] = jnp.where(low_lane[:v // 2], box_up[:v // 2], box_up[v // 2:])

    wides = (cw, lw, mw)

    def halo(kind, side):
        wide = wides[kind]
        return pltpu.make_async_remote_copy(
            src_ref=wide.at[1], dst_ref=wide.at[2 - 2 * side], send_sem=halo_send.at[2 * kind + side],
            recv_sem=halo_recv.at[2 * kind + side], device_id=(me - 1 + 2 * side,),
            device_id_type=pl.DeviceIdType.MESH)

    def halo_starts(kind):
        @pl.when(me > 0)
        def _():
            halo(kind, 0).start()

        @pl.when(me < n - 1)
        def _():
            halo(kind, 1).start()

    def halo_arrive(kind):
        wide = wides[kind]

        @pl.when(me < n - 1)
        def _():
            halo(kind, 0).wait_recv()

        @pl.when(me > 0)
        def _():
            halo(kind, 1).wait_recv()

        @pl.when(me == 0)
        def _():
            wide[0] = jnp.zeros(wide.shape[1:], BF16)

        @pl.when(me == n - 1)
        def _():
            wide[2] = jnp.zeros(wide.shape[1:], BF16)

    def halo_sent(kind):
        @pl.when(me > 0)
        def _():
            halo(kind, 0).wait_send()

        @pl.when(me < n - 1)
        def _():
            halo(kind, 1).wait_send()

    def everyone(step):
        other = lax.rem(me + step, n)
        return pltpu.make_async_remote_copy(
            src_ref=gathered.at[me], dst_ref=gathered.at[me], send_sem=all_send.at[0],
            recv_sem=all_recv.at[0], device_id=(other,), device_id_type=pl.DeviceIdType.MESH)

    def send_step(step, carry):
        everyone(step).start()
        return carry

    def send_all():
        told(bits - 1)
        lax.fori_loop(1, n, send_step, 0)

    pl.semaphore_wait(barrier, bits + has_beside.astype(jnp.int32))

    tell(1)
    halo_starts(1)
    halo_starts(0)
    halo_starts(2)

    for i in (8, 9, 10):
        loads[i].wait()
    near_raw[...] = near_raw[...] & (4 * leaves - 1)
    far_raw[...] = far_raw[...] & (4 * leaves - 1)
    mid_raw[...] = mid_raw[...] & (4 * groups - 1)
    index_copies = [pltpu.make_async_copy(a, b, index_sem.at[i]) for i, (a, b) in enumerate(
        ((near_raw, near_source), (far_raw, far_source), (mid_raw, mid_source)))]
    for copy in index_copies:
        copy.start()

    told(1)
    tell(2)
    loads[11].wait()
    loads[12].wait()
    count = near_count[...]
    leaf_row = rows((leaves, LANES))
    slot_lane = lanes((leaves, LANES))
    assignment = []
    for b in range(capacity // LANES):
        hit = (leaf_row == near_target[b:b + 1, :]) & (slot_lane + b * LANES < count)
        assignment.append(jnp.where(hit, 1.0, 0.0).astype(BF16))
    strips = side // LANES
    for b in range(strips // 2):
        low = jnp.concatenate(assignment[2 * b:2 * b + 2], axis=1)
        high = jnp.concatenate(assignment[strips + 2 * b:strips + 2 * b + 2], axis=1)
        assigned[b] = jnp.concatenate([low, high], axis=0)
    for bit in range(2, bits - 1):
        told(bit)
        tell(bit + 1)

    @pl.when(me >= n // 2)
    def _():
        send_all()

    def put(tiles, slot, value):
        tiles[slot] = value

    def take(tiles, slot):
        return tiles[slot]

    def spread_pairs(wide, tiles, per_box, box):
        x = wide[box].astype(F32)
        first = lax.rem(me + 3 + box, 4) * per_box
        for t in range(per_box // 2):
            tile = x[:, t * LANES:(t + 1) * LANES]
            turned = pltpu.roll(tile, LANES // 2, 1)
            put(tiles, first + 2 * t, jnp.where(half, tile, turned))
            put(tiles, first + 2 * t + 1, jnp.where(half, turned, tile))

    fold = LANES // r0
    lane_block = lanes((v, LANES)) // r0

    def spread_leaves(box):
        x = lw[box].astype(F32)
        first = lax.rem(me + 3 + box, 4) * leaves
        for t in range(leaves // fold):
            tile = x[:, t * LANES:(t + 1) * LANES]
            turned = [tile] + [pltpu.roll(tile, r0 * k, 1) for k in range(1, fold)]
            for p in range(fold):
                piece = turned[(0 - p) % fold]
                for w in range(1, fold):
                    piece = jnp.where(lane_block == w, turned[(w - p) % fold], piece)
                put(leaf_tiles, first + t * fold + p, piece)

    for tiles, per_box in ((charge_tiles, leaves), (leaf_tiles, leaves), (mid_tiles, groups)):
        unused = pl.ds(lax.rem(me + 2, 4) * per_box, per_box)
        tiles[unused] = jnp.zeros((per_box, v, LANES), F32)
    spread_pairs(cw, charge_tiles, leaves, 1)
    spread_leaves(1)
    spread_pairs(mw, mid_tiles, groups, 1)

    loads[6].wait()
    loads[7].wait()
    for copy in tops:
        copy.wait()
    offsets = []
    offset = 0
    for level in range(levels + 1):
        offsets.append(offset)
        offset += (n >> level) // 2 + 1
    wide_low = lanes((r, LANES)) < r
    diagonal_lane = lanes((r, LANES)) - rows((r, LANES))
    chain = None
    pushed = []
    for level in range(levels + 1):
        cluster = me >> level
        odd = lax.rem(cluster, 2)
        if level == 0:
            q = box_coupling[...].astype(F32)
        else:
            q = dot_nn(chain[:, :r].astype(BF16), top_coupling[level - 1])
        pair = q[:, :LANES]
        turned = pltpu.roll(pair, LANES // 2, 1)
        third = jnp.concatenate([q[:, LANES:], q[:, LANES:]], axis=1)
        is_odd = odd.astype(F32)
        before = jnp.where(wide_low, pair, pair * is_odd)
        after = jnp.where(wide_low, turned * (1.0 - is_odd), third)
        pushed.append((before.astype(BF16), after.astype(BF16)))
        if level < levels:
            t = top_transfer[n - (n >> level) + (cluster >> 1)]
            t = jnp.concatenate([t, t], axis=0)
            if level == 0:
                lhs = jnp.where(diagonal_lane == r * odd, 1.0, 0.0)
            else:
                lhs = jnp.where(wide_low, chain * (1.0 - is_odd), chain * is_odd)
            chain = dot_nt(lhs.astype(BF16), t)
    blank = jnp.zeros((r, LANES), BF16)
    for level in range(levels, -1, -1):
        tiles = (n >> level) // 2
        if level == levels:
            for tile in range(tiles):
                weights[offsets[level] + tile] = blank
        else:
            above = n - (n >> level)
            for tile in range(tiles // 2):
                zero_block = jnp.zeros((r, 2 * r), BF16)
                matrix = jnp.concatenate([
                    jnp.concatenate([top_transfer[above + 2 * tile], zero_block], axis=1),
                    jnp.concatenate([zero_block, top_transfer[above + 2 * tile + 1]], axis=1)], axis=0)
                out = dot_nn(weights[offsets[level + 1] + tile], matrix).astype(BF16)
                weights[offsets[level] + 2 * tile] = out[:, :LANES]
                weights[offsets[level] + 2 * tile + 1] = out[:, LANES:]
        own = me >> (level + 1)
        weights[offsets[level] + jnp.where(own > 0, own - 1, tiles)] = pushed[level][0]
        weights[offsets[level] + jnp.where(own + 1 < tiles, own + 1, tiles)] = pushed[level][1]

    for copy in index_copies:
        copy.wait()
    halo_arrive(1)
    spread_leaves(0)
    spread_leaves(2)
    loads[5].wait()

    def far_step(c, carry):
        parts = []
        for l in range(child):
            tiles = []
            for t in range(k0 // fold):
                piece = take(leaf_tiles, far_source[t * fold, c * child + l])
                for w in range(1, fold):
                    piece = jnp.where(lane_block == w, take(leaf_tiles, far_source[t * fold + w, c * child + l]), piece)
                tiles.append(piece)
            parts.append(jnp.concatenate(tiles, axis=1))
        lhs = jnp.concatenate(parts, axis=0).astype(BF16)
        matrix = far_coupling[c * child:(c + 1) * child].reshape(child * r0, k0 * r0)
        leaf_far[c] = diagonal(dot_nt(lhs, matrix), v, r0)
        return carry

    for c in range(groups):
        far_step(c, 0)

    @pl.when(me < n // 2)
    def _():
        send_all()

    halo_arrive(0)
    spread_pairs(cw, charge_tiles, leaves, 0)
    spread_pairs(cw, charge_tiles, leaves, 2)

    zero = jnp.zeros((2 * v, LANES), F32)

    def gather(first):
        pieces = []
        for i in range(4):
            slot = first + i
            x = take(charge_tiles, near_source[slot // LANES, slot % LANES])
            pieces.append(jnp.where(half, x, 0.0) if i % 2 == 0 else jnp.where(half, 0.0, x))
        upper = jnp.concatenate([pieces[0], pieces[1]], axis=0)
        lower = jnp.concatenate([pieces[2], pieces[3]], axis=0)
        return jnp.concatenate(
            [jnp.concatenate([upper, zero], axis=1), jnp.concatenate([zero, lower], axis=1)], axis=0).astype(BF16)

    def collect(b, u):
        c = contribution[pl.ds(b * 2 * LANES * v + u, 2 * LANES, stride=v), :]
        return dot_nn(assigned[b], c.astype(BF16))

    steps = side // 4
    spans = side // (2 * LANES)
    per_span = steps // spans
    every = per_span // v
    wide_half = lanes((leaves, LANES)) < m
    mixed_half = lanes((4 * v, LANES)) < m
    for g in range(steps):
        if g % (steps // CHUNKS) == 0:
            near_load(g // (steps // CHUNKS), 0).wait()
            near_load(g // (steps // CHUNKS), 1).wait()
        lhs = jnp.concatenate([gather(g * 4), gather(side + g * 4)], axis=0)
        block = jnp.concatenate([
            near_blocks[:, g * 4 * m:(g + 1) * 4 * m],
            near_blocks[:, (side + g * 4) * m:(side + (g + 1) * 4) * m]], axis=0)
        out = dot_nt(lhs, block)
        contribution[g * 4 * v:(g + 1) * 4 * v, :] = jnp.where(mixed_half, out[:4 * v], out[4 * v:])
        span = g // per_span
        if span > 0 and g % every == every - 1:
            u = g % per_span // every
            part = collect(span - 1, u)
            near_part[u] = part if span == 1 else near_part[u] + part

    for u in range(v):
        total = collect(spans - 1, u)
        if spans > 1:
            total = total + near_part[u]
        mixed = jnp.where(wide_half, total[:leaves], total[leaves:])
        near_rows[u * leaves:(u + 1) * leaves, :] = mixed + pltpu.roll(mixed, LANES // 2, 1)

    halo_arrive(2)
    spread_pairs(mw, mid_tiles, groups, 0)
    spread_pairs(mw, mid_tiles, groups, 2)
    loads[4].wait()
    for g in range(groups // quad):
        parts = []
        for c in range(g * quad, (g + 1) * quad):
            tiles = []
            for t in range(k1 // 2):
                a = take(mid_tiles, mid_source[c, 2 * t])
                b = take(mid_tiles, mid_source[c, 2 * t + 1])
                tiles.append(jnp.where(half, a, b))
            parts.append(jnp.concatenate(tiles, axis=1))
        lhs = jnp.concatenate(parts, axis=0).astype(BF16)
        matrix = mid_coupling[g * quad:(g + 1) * quad].reshape(quad * r, k1 * r)
        mid_far[:, g * quad * r:(g + 1) * quad * r] = diagonal(dot_nt(lhs, matrix), v, r)

    quad_mask = (rows((4 * r0, 4 * m)) // r0 == lanes((4 * r0, 4 * m)) // m).astype(F32).astype(BF16)
    pad = jnp.zeros((v, LANES), F32)
    tall_low = lanes((r + 2 * v, LANES)) < r
    for pair in range(groups // 2):
        span = slice(pair * LANES, (pair + 1) * LANES)
        tile = jnp.concatenate([mid_transfer[:, span].astype(F32), mid_far[:, span], pad], axis=0)
        lhs = jnp.concatenate([jnp.where(tall_low, tile, 0.0), jnp.where(tall_low, 0.0, tile)], axis=0).astype(BF16)
        push = dot_nn(lhs, leaf_transfer[2 * pair:2 * pair + 2].reshape(2 * r, child * r0))
        for s in range(2):
            c = 2 * pair + s
            one = push[s * (r + 2 * v):(s + 1) * (r + 2 * v)]
            lhs = jnp.concatenate([one[:r], one[r:r + v] + leaf_far[c], one[r + v:]], axis=0).astype(BF16)
            for h in range(child // 4):
                q = c * (child // 4) + h
                b = jnp.concatenate([basis[:, q * 4 * m:(q + 1) * 4 * m]] * 4, axis=0) * quad_mask
                far = dot_nn(lhs[:, h * 4 * r0:(h + 1) * 4 * r0], b)
                response[:, q * 4 * m:(q + 1) * 4 * m] = far[:r].astype(BF16)
                for w in range(2):
                    leaf = q * 4 + 2 * w
                    even = near_rows[pl.ds(leaf, v, stride=leaves), :]
                    odd = near_rows[pl.ds(leaf + 1, v, stride=leaves), :]
                    base[:, leaf * m:(leaf + 2) * m] = (
                        far[r:r + v, w * LANES:(w + 1) * LANES] + jnp.where(half, even, odd))

    others = gathered.at[pl.ds(0, n - 1)]
    pltpu.make_async_copy(others, others, all_recv.at[0]).wait()
    low_half = low_lane[:v // 2]
    lhs = []
    for tile in range(n // 2):
        a = gathered[2 * tile]
        b = gathered[2 * tile + 1]
        lhs.append(jnp.concatenate([
            jnp.where(low_half, a, pltpu.roll(b, LANES // 2, 1)),
            jnp.where(low_half, pltpu.roll(a, LANES // 2, 1), b)], axis=0))
    lhs = jnp.concatenate(lhs, axis=1).astype(BF16)
    downward = dot_nt(lhs, jnp.concatenate([weights[tile] for tile in range(n // 2)], axis=1)).astype(BF16)
    for q in range(leaves // 4):
        span = slice(q * 4 * m, (q + 1) * 4 * m)
        out_ref[:, span] = (base[:, span] + dot_nn(downward, response[:, span])).astype(BF16)

    pltpu.make_async_copy(others, others, all_send.at[0]).wait()
    for kind in range(3):
        halo_sent(kind)


def body(
    charges, leaf_basis, leaf_transfer, mid_transfer, far_source, far_coupling, mid_source, mid_coupling,
    box_coupling, top_transfer, top_coupling, near_target, near_source, near_count, near_blocks,
):
    n = lax.axis_size(AXIS)
    v, points = charges.shape
    leaves, k0 = far_source.shape
    m = points // leaves
    r0 = leaf_basis.shape[0]
    groups, k1 = mid_source.shape
    r = leaf_transfer.shape[1]
    capacity = near_target.shape[0]
    levels = (n // 4).bit_length() - 1
    bits = n.bit_length() - 1
    tiles = sum((n >> level) // 2 + 1 for level in range(levels + 1))
    sizes = (v, leaves, m, r0, groups, r, k0, k1, capacity)
    vmem = pl.BlockSpec(memory_space=pltpu.VMEM)
    hbm = pl.BlockSpec(memory_space=pltpu.HBM)
    dma = pltpu.SemaphoreType.DMA
    return pl.pallas_call(
        functools.partial(kernel, n, sizes),
        out_shape=pltpu.VMEM(charges.shape, BF16),
        in_specs=[hbm] * 3 + [pl.BlockSpec(memory_space=pl.ANY)] + [hbm] * 11,
        out_specs=vmem,
        scratch_shapes=[
            pltpu.VMEM((3, v, points), BF16),
            pltpu.VMEM((3, v, leaves * r0), BF16),
            pltpu.VMEM((3, v, groups * r), BF16),
            pltpu.VMEM((n, v // 2, 2 * r), F32),
            pltpu.VMEM(leaf_basis.shape, BF16),
            pltpu.VMEM(leaf_transfer.shape, BF16),
            pltpu.VMEM(mid_transfer.shape[1:], BF16),
            pltpu.VMEM(far_coupling.shape, BF16),
            pltpu.VMEM(mid_coupling.shape, BF16),
            pltpu.VMEM(box_coupling.shape[1:], BF16),
            pltpu.VMEM(top_transfer.shape, BF16),
            pltpu.VMEM((levels,) + top_coupling.shape[1:], BF16),
            pltpu.VMEM(near_blocks.shape, BF16),
            pltpu.VMEM((capacity // LANES, LANES), jnp.int32),
            pltpu.VMEM((k0, leaves), jnp.int32),
            pltpu.VMEM((groups, k1), jnp.int32),
            pltpu.VMEM((capacity // LANES, LANES), jnp.int32),
            pltpu.SMEM((capacity // LANES, LANES), jnp.int32),
            pltpu.SMEM((k0, leaves), jnp.int32),
            pltpu.SMEM((groups, k1), jnp.int32),
            pltpu.VMEM((1, 1), jnp.int32),
            pltpu.VMEM((4 * leaves, v, LANES), F32),
            pltpu.VMEM((4 * leaves, v, LANES), F32),
            pltpu.VMEM((4 * groups, v, LANES), F32),
            pltpu.VMEM((capacity // 2 * v, 2 * m), F32),
            pltpu.VMEM((v, 2 * leaves, 2 * m), F32),
            pltpu.VMEM((v * leaves, 2 * m), F32),
            pltpu.VMEM((groups, v, leaves // groups * r0), F32),
            pltpu.VMEM((v, groups * r), F32),
            pltpu.VMEM((tiles, r, 2 * r), BF16),
            pltpu.VMEM((r, points), BF16),
            pltpu.VMEM((v, points), F32),
            pltpu.VMEM((capacity // LANES // 4, 2 * leaves, 2 * LANES), BF16),
            dma((13,)),
            dma((2 * CHUNKS,)),
            dma((levels,)),
            dma((3,)),
            dma((6,)),
            dma((6,)),
            dma((1,)),
            dma((1,)),
            pltpu.SemaphoreType.REGULAR((bits,)),
        ],
        compiler_params=pltpu.CompilerParams(
            collective_id=0, has_side_effects=True, vmem_limit_bytes=60 * 1024 * 1024),
    )(
        near_source.reshape(capacity // LANES, LANES), far_source.T, mid_source, near_count.reshape(1, 1), near_target.reshape(capacity // LANES, LANES),
        charges, leaf_basis, leaf_transfer, mid_transfer, far_coupling, mid_coupling,
        box_coupling, top_transfer, top_coupling, near_blocks,
    )


def solution(mesh):
    c = "clusters"
    in_specs = (
        P(None, c), P(None, c), P(c, None, None), P(c, None, None), P(c, None), P(c, None, None),
        P(c, None), P(c, None, None), P(c, None, None), P(), P(), P(c), P(c), P(c), P(None, c),
    )
    return jax.shard_map(body, mesh=mesh, in_specs=in_specs, out_specs=P(None, c), check_vma=False)
```

```python
import functools

import jax
import jax.numpy as jnp
from jax import lax
from jax.experimental import pallas as pl
from jax.experimental.pallas import tpu as pltpu
from jax.sharding import PartitionSpec as P

F32 = jnp.float32
BF16 = jnp.bfloat16
AXIS = "clusters"
NT = (((1,), (1,)), ((), ()))
NN = (((1,), (0,)), ((), ()))
LANES = 128
CHUNKS = 8
PASS_AT = 2


def dot_nt(a, b):
    return lax.dot_general(a, b, NT, preferred_element_type=F32)


def dot_nn(a, b):
    return lax.dot_general(a, b, NN, preferred_element_type=F32)


def lanes(shape):
    return lax.broadcasted_iota(jnp.int32, shape, len(shape) - 1)


def rows(shape):
    return lax.broadcasted_iota(jnp.int32, shape, len(shape) - 2)


def diagonal(out, v, width):
    blocks = out.shape[0] // v
    lane = lanes((v, out.shape[1])) // width
    total = jnp.zeros((v, out.shape[1]), F32)
    for block in range(blocks):
        total = jnp.where(lane == block, out[block * v:(block + 1) * v], total)
    return total


def kernel(
    n, sizes,
    near_source_h, far_source_h, mid_source_h, near_count_h, near_target_h,
    charges_h, basis_h, leaf_transfer_h, mid_transfer_h, far_coupling_h, mid_coupling_h,
    box_coupling_h, top_transfer_h, top_coupling_h, near_blocks_h,
    out_ref,
    cw, lw, mw, gathered, basis, leaf_transfer, mid_transfer, far_coupling, mid_coupling,
    box_coupling, top_transfer, top_coupling, near_blocks,
    near_raw, far_raw, mid_raw, near_target, near_source, far_source, mid_source, near_count,
    charge_tiles, leaf_tiles, mid_tiles, contribution, near_part, near_rows, leaf_far, mid_far, weights, response, base,
    assigned,
    load_sem, near_sem, top_sem, index_sem, halo_send, halo_recv, all_send, all_recv,
):
    v, leaves, m, r0, groups, r, k0, k1, capacity = sizes
    child = leaves // groups
    levels = (n // 4).bit_length() - 1
    across_layers = min(4, n)
    in_layer = n // across_layers
    me = lax.axis_index(AXIS)
    layer, place = me // in_layer, lax.rem(me, in_layer)
    half = lanes((v, LANES)) < m
    low_lane = lanes((v, LANES)) < r

    barrier = pltpu.get_barrier_semaphore()

    pairs = [
        (charges_h, cw.at[1]), (basis_h, basis), (leaf_transfer_h, leaf_transfer), (mid_transfer_h.at[0], mid_transfer),
        (mid_coupling_h, mid_coupling), (far_coupling_h, far_coupling), (box_coupling_h.at[0], box_coupling),
        (top_transfer_h, top_transfer), (near_source_h, near_raw), (far_source_h, far_raw), (mid_source_h, mid_raw),
        (near_target_h, near_target), (near_count_h, near_count),
    ]
    loads = [pltpu.make_async_copy(s, d, load_sem.at[i]) for i, (s, d) in enumerate(pairs)]
    side = capacity // 2
    width = side * m // CHUNKS

    def near_load(chunk, part):
        span = pl.ds(part * side * m + chunk * width, width)
        return pltpu.make_async_copy(
            near_blocks_h.at[:, span], near_blocks.at[:, span], near_sem.at[2 * chunk + part])

    tops = []
    for level in range(1, levels + 1):
        start = n - (n >> (level - 1))
        tops.append(pltpu.make_async_copy(
            top_coupling_h.at[start + (me >> level)], top_coupling.at[level - 1], top_sem.at[level - 1]))

    for i in (0, 1, 2, 3, 8, 9, 10, 11, 12, 6, 7):
        loads[i].start()
    for copy in tops:
        copy.start()
    loads[5].start()
    for chunk in range(CHUNKS):
        near_load(chunk, 0).start()
        near_load(chunk, 1).start()
    loads[4].start()

    def above(step):
        return lax.rem(layer + step, across_layers) * in_layer + place

    def around(step):
        return layer * in_layer + lax.rem(place + step, in_layer)

    beside = jnp.where(place == 0, me - 1, me + 1)
    has_beside = ((place == 0) | (place == in_layer - 1)) & (beside >= 0) & (beside < n)

    def greet(other):
        pl.semaphore_signal(barrier, inc=1, device_id=(other,), device_id_type=pl.DeviceIdType.MESH)

    for step in range(1, across_layers):
        greet(above(step))

    def greet_around(step, carry):
        greet(around(step))
        return carry

    lax.fori_loop(1, in_layer, greet_around, 0)

    @pl.when(has_beside)
    def _():
        greet(beside)

    loads[0].wait()
    loads[1].wait()
    span_points = child * m
    lane_leaf = lanes((v, span_points)) // m
    ups = []
    for c in range(groups):
        x = cw[1, :, c * span_points:(c + 1) * span_points].astype(F32)
        lhs = jnp.concatenate([jnp.where(lane_leaf == l, x, 0.0) for l in range(child)], axis=0).astype(BF16)
        b = basis[:, c * span_points:(c + 1) * span_points]
        up = diagonal(dot_nt(lhs, jnp.concatenate([b] * child, axis=0)), v, r0).astype(BF16)
        lw[1, :, c * child * r0:(c + 1) * child * r0] = up
        ups.append(up.astype(F32))
    loads[2].wait()
    loads[3].wait()
    quad = 4
    for g in range(groups // quad):
        lhs = jnp.concatenate(ups[g * quad:(g + 1) * quad], axis=0).astype(BF16)
        matrix = leaf_transfer[g * quad:(g + 1) * quad].reshape(quad * r, child * r0)
        mw[1, :, g * quad * r:(g + 1) * quad * r] = diagonal(dot_nt(lhs, matrix), v, r).astype(BF16)
    transfer = mid_transfer[...]
    box_up = dot_nt(mw[1], jnp.concatenate([transfer, transfer], axis=0))
    gathered[place * across_layers + layer] = jnp.where(low_lane[:v // 2], box_up[:v // 2], box_up[v // 2:])

    wides = (cw, lw, mw)

    def halo(kind, side):
        wide = wides[kind]
        return pltpu.make_async_remote_copy(
            src_ref=wide.at[1], dst_ref=wide.at[2 - 2 * side], send_sem=halo_send.at[2 * kind + side],
            recv_sem=halo_recv.at[2 * kind + side], device_id=(me - 1 + 2 * side,),
            device_id_type=pl.DeviceIdType.MESH)

    def halo_starts(kind):
        @pl.when(me > 0)
        def _():
            halo(kind, 0).start()

        @pl.when(me < n - 1)
        def _():
            halo(kind, 1).start()

    def halo_arrive(kind):
        wide = wides[kind]

        @pl.when(me < n - 1)
        def _():
            halo(kind, 0).wait_recv()

        @pl.when(me > 0)
        def _():
            halo(kind, 1).wait_recv()

        @pl.when(me == 0)
        def _():
            wide[0] = jnp.zeros(wide.shape[1:], BF16)

        @pl.when(me == n - 1)
        def _():
            wide[2] = jnp.zeros(wide.shape[1:], BF16)

    def halo_sent(kind):
        @pl.when(me > 0)
        def _():
            halo(kind, 0).wait_send()

        @pl.when(me < n - 1)
        def _():
            halo(kind, 1).wait_send()

    def rise(step):
        own = gathered.at[place * across_layers + layer]
        return pltpu.make_async_remote_copy(
            src_ref=own, dst_ref=own, send_sem=all_send.at[0], recv_sem=all_recv.at[0],
            device_id=(above(step),), device_id_type=pl.DeviceIdType.MESH)

    def share(step):
        own = gathered.at[pl.ds(place * across_layers, across_layers)]
        return pltpu.make_async_remote_copy(
            src_ref=own, dst_ref=own, send_sem=all_send.at[1], recv_sem=all_recv.at[1],
            device_id=(around(step),), device_id_type=pl.DeviceIdType.MESH)

    def share_step(step, carry):
        share(step).start()
        return carry

    def take_all(sems, stage):
        count = (across_layers - 1, (in_layer - 1) * across_layers)[stage]
        block = gathered.at[pl.ds(0, count)]
        pltpu.make_async_copy(block, block, sems.at[stage]).wait()

    def pass_on():
        take_all(all_recv, 0)
        lax.fori_loop(1, in_layer, share_step, 0)

    pl.semaphore_wait(barrier, across_layers + in_layer - 2 + has_beside.astype(jnp.int32))

    for step in range(1, across_layers):
        rise(step).start()
    halo_starts(1)
    halo_starts(0)
    halo_starts(2)

    for i in (8, 9, 10):
        loads[i].wait()
    near_raw[...] = near_raw[...] & (4 * leaves - 1)
    far_raw[...] = far_raw[...] & (4 * leaves - 1)
    mid_raw[...] = mid_raw[...] & (4 * groups - 1)
    index_copies = [pltpu.make_async_copy(a, b, index_sem.at[i]) for i, (a, b) in enumerate(
        ((near_raw, near_source), (far_raw, far_source), (mid_raw, mid_source)))]
    for copy in index_copies:
        copy.start()

    loads[11].wait()
    loads[12].wait()
    count = near_count[...]
    leaf_row = rows((leaves, LANES))
    slot_lane = lanes((leaves, LANES))
    assignment = []
    for b in range(capacity // LANES):
        hit = (leaf_row == near_target[b:b + 1, :]) & (slot_lane + b * LANES < count)
        assignment.append(jnp.where(hit, 1.0, 0.0).astype(BF16))
    strips = side // LANES
    for b in range(strips // 2):
        low = jnp.concatenate(assignment[2 * b:2 * b + 2], axis=1)
        high = jnp.concatenate(assignment[strips + 2 * b:strips + 2 * b + 2], axis=1)
        assigned[b] = jnp.concatenate([low, high], axis=0)
    def put(tiles, slot, value):
        tiles[slot] = value

    def take(tiles, slot):
        return tiles[slot]

    def spread_pairs(wide, tiles, per_box, box):
        x = wide[box].astype(F32)
        first = lax.rem(me + 3 + box, 4) * per_box
        for t in range(per_box // 2):
            tile = x[:, t * LANES:(t + 1) * LANES]
            turned = pltpu.roll(tile, LANES // 2, 1)
            put(tiles, first + 2 * t, jnp.where(half, tile, turned))
            put(tiles, first + 2 * t + 1, jnp.where(half, turned, tile))

    fold = LANES // r0
    lane_block = lanes((v, LANES)) // r0

    def spread_leaves(box):
        x = lw[box].astype(F32)
        first = lax.rem(me + 3 + box, 4) * leaves
        for t in range(leaves // fold):
            tile = x[:, t * LANES:(t + 1) * LANES]
            turned = [tile] + [pltpu.roll(tile, r0 * k, 1) for k in range(1, fold)]
            for p in range(fold):
                piece = turned[(0 - p) % fold]
                for w in range(1, fold):
                    piece = jnp.where(lane_block == w, turned[(w - p) % fold], piece)
                put(leaf_tiles, first + t * fold + p, piece)

    for tiles, per_box in ((charge_tiles, leaves), (leaf_tiles, leaves), (mid_tiles, groups)):
        unused = pl.ds(lax.rem(me + 2, 4) * per_box, per_box)
        tiles[unused] = jnp.zeros((per_box, v, LANES), F32)
    spread_pairs(cw, charge_tiles, leaves, 1)
    spread_leaves(1)
    spread_pairs(mw, mid_tiles, groups, 1)

    loads[6].wait()
    loads[7].wait()
    for copy in tops:
        copy.wait()
    offsets = []
    offset = 0
    for level in range(levels + 1):
        offsets.append(offset)
        offset += (n >> level) // 2 + 1
    wide_low = lanes((r, LANES)) < r
    diagonal_lane = lanes((r, LANES)) - rows((r, LANES))
    chain = None
    pushed = []
    for level in range(levels + 1):
        cluster = me >> level
        odd = lax.rem(cluster, 2)
        if level == 0:
            q = box_coupling[...].astype(F32)
        else:
            q = dot_nn(chain[:, :r].astype(BF16), top_coupling[level - 1])
        pair = q[:, :LANES]
        turned = pltpu.roll(pair, LANES // 2, 1)
        third = jnp.concatenate([q[:, LANES:], q[:, LANES:]], axis=1)
        is_odd = odd.astype(F32)
        before = jnp.where(wide_low, pair, pair * is_odd)
        after = jnp.where(wide_low, turned * (1.0 - is_odd), third)
        pushed.append((before.astype(BF16), after.astype(BF16)))
        if level < levels:
            t = top_transfer[n - (n >> level) + (cluster >> 1)]
            t = jnp.concatenate([t, t], axis=0)
            if level == 0:
                lhs = jnp.where(diagonal_lane == r * odd, 1.0, 0.0)
            else:
                lhs = jnp.where(wide_low, chain * (1.0 - is_odd), chain * is_odd)
            chain = dot_nt(lhs.astype(BF16), t)
    blank = jnp.zeros((r, LANES), BF16)
    for level in range(levels, -1, -1):
        tiles = (n >> level) // 2
        if level == levels:
            for tile in range(tiles):
                weights[offsets[level] + tile] = blank
        else:
            above = n - (n >> level)
            for tile in range(tiles // 2):
                zero_block = jnp.zeros((r, 2 * r), BF16)
                matrix = jnp.concatenate([
                    jnp.concatenate([top_transfer[above + 2 * tile], zero_block], axis=1),
                    jnp.concatenate([zero_block, top_transfer[above + 2 * tile + 1]], axis=1)], axis=0)
                out = dot_nn(weights[offsets[level + 1] + tile], matrix).astype(BF16)
                weights[offsets[level] + 2 * tile] = out[:, :LANES]
                weights[offsets[level] + 2 * tile + 1] = out[:, LANES:]
        own = me >> (level + 1)
        weights[offsets[level] + jnp.where(own > 0, own - 1, tiles)] = pushed[level][0]
        weights[offsets[level] + jnp.where(own + 1 < tiles, own + 1, tiles)] = pushed[level][1]

    for copy in index_copies:
        copy.wait()
    halo_arrive(1)
    spread_leaves(0)
    spread_leaves(2)
    loads[5].wait()

    def far_step(c, carry):
        parts = []
        for l in range(child):
            tiles = []
            for t in range(k0 // fold):
                piece = take(leaf_tiles, far_source[t * fold, c * child + l])
                for w in range(1, fold):
                    piece = jnp.where(lane_block == w, take(leaf_tiles, far_source[t * fold + w, c * child + l]), piece)
                tiles.append(piece)
            parts.append(jnp.concatenate(tiles, axis=1))
        lhs = jnp.concatenate(parts, axis=0).astype(BF16)
        matrix = far_coupling[c * child:(c + 1) * child].reshape(child * r0, k0 * r0)
        leaf_far[c] = diagonal(dot_nt(lhs, matrix), v, r0)
        return carry

    for c in range(groups):
        far_step(c, 0)

    halo_arrive(0)
    spread_pairs(cw, charge_tiles, leaves, 0)
    spread_pairs(cw, charge_tiles, leaves, 2)

    zero = jnp.zeros((2 * v, LANES), F32)

    def gather(first):
        pieces = []
        for i in range(4):
            slot = first + i
            x = take(charge_tiles, near_source[slot // LANES, slot % LANES])
            pieces.append(jnp.where(half, x, 0.0) if i % 2 == 0 else jnp.where(half, 0.0, x))
        upper = jnp.concatenate([pieces[0], pieces[1]], axis=0)
        lower = jnp.concatenate([pieces[2], pieces[3]], axis=0)
        return jnp.concatenate(
            [jnp.concatenate([upper, zero], axis=1), jnp.concatenate([zero, lower], axis=1)], axis=0).astype(BF16)

    def collect(b, u):
        c = contribution[pl.ds(b * 2 * LANES * v + u, 2 * LANES, stride=v), :]
        return dot_nn(assigned[b], c.astype(BF16))

    steps = side // 4
    spans = side // (2 * LANES)
    per_span = steps // spans
    every = per_span // v
    wide_half = lanes((leaves, LANES)) < m
    mixed_half = lanes((4 * v, LANES)) < m
    for g in range(steps):
        if g == PASS_AT * steps // 8:
            pass_on()
        if g % (steps // CHUNKS) == 0:
            near_load(g // (steps // CHUNKS), 0).wait()
            near_load(g // (steps // CHUNKS), 1).wait()
        lhs = jnp.concatenate([gather(g * 4), gather(side + g * 4)], axis=0)
        block = jnp.concatenate([
            near_blocks[:, g * 4 * m:(g + 1) * 4 * m],
            near_blocks[:, (side + g * 4) * m:(side + (g + 1) * 4) * m]], axis=0)
        out = dot_nt(lhs, block)
        contribution[g * 4 * v:(g + 1) * 4 * v, :] = jnp.where(mixed_half, out[:4 * v], out[4 * v:])
        span = g // per_span
        if span > 0 and g % every == every - 1:
            u = g % per_span // every
            part = collect(span - 1, u)
            near_part[u] = part if span == 1 else near_part[u] + part

    for u in range(v):
        total = collect(spans - 1, u)
        if spans > 1:
            total = total + near_part[u]
        mixed = jnp.where(wide_half, total[:leaves], total[leaves:])
        near_rows[u * leaves:(u + 1) * leaves, :] = mixed + pltpu.roll(mixed, LANES // 2, 1)

    halo_arrive(2)
    spread_pairs(mw, mid_tiles, groups, 0)
    spread_pairs(mw, mid_tiles, groups, 2)
    loads[4].wait()
    for g in range(groups // quad):
        parts = []
        for c in range(g * quad, (g + 1) * quad):
            tiles = []
            for t in range(k1 // 2):
                a = take(mid_tiles, mid_source[c, 2 * t])
                b = take(mid_tiles, mid_source[c, 2 * t + 1])
                tiles.append(jnp.where(half, a, b))
            parts.append(jnp.concatenate(tiles, axis=1))
        lhs = jnp.concatenate(parts, axis=0).astype(BF16)
        matrix = mid_coupling[g * quad:(g + 1) * quad].reshape(quad * r, k1 * r)
        mid_far[:, g * quad * r:(g + 1) * quad * r] = diagonal(dot_nt(lhs, matrix), v, r)

    quad_mask = (rows((4 * r0, 4 * m)) // r0 == lanes((4 * r0, 4 * m)) // m).astype(F32).astype(BF16)
    pad = jnp.zeros((v, LANES), F32)
    tall_low = lanes((r + 2 * v, LANES)) < r
    for pair in range(groups // 2):
        span = slice(pair * LANES, (pair + 1) * LANES)
        tile = jnp.concatenate([mid_transfer[:, span].astype(F32), mid_far[:, span], pad], axis=0)
        lhs = jnp.concatenate([jnp.where(tall_low, tile, 0.0), jnp.where(tall_low, 0.0, tile)], axis=0).astype(BF16)
        push = dot_nn(lhs, leaf_transfer[2 * pair:2 * pair + 2].reshape(2 * r, child * r0))
        for s in range(2):
            c = 2 * pair + s
            one = push[s * (r + 2 * v):(s + 1) * (r + 2 * v)]
            lhs = jnp.concatenate([one[:r], one[r:r + v] + leaf_far[c], one[r + v:]], axis=0).astype(BF16)
            for h in range(child // 4):
                q = c * (child // 4) + h
                b = jnp.concatenate([basis[:, q * 4 * m:(q + 1) * 4 * m]] * 4, axis=0) * quad_mask
                far = dot_nn(lhs[:, h * 4 * r0:(h + 1) * 4 * r0], b)
                response[:, q * 4 * m:(q + 1) * 4 * m] = far[:r].astype(BF16)
                for w in range(2):
                    leaf = q * 4 + 2 * w
                    even = near_rows[pl.ds(leaf, v, stride=leaves), :]
                    odd = near_rows[pl.ds(leaf + 1, v, stride=leaves), :]
                    base[:, leaf * m:(leaf + 2) * m] = (
                        far[r:r + v, w * LANES:(w + 1) * LANES] + jnp.where(half, even, odd))

    take_all(all_recv, 1)

    def box(b):
        return gathered[b % in_layer * across_layers + b // in_layer]

    low_half = low_lane[:v // 2]
    lhs = []
    for tile in range(n // 2):
        a = box(2 * tile)
        b = box(2 * tile + 1)
        lhs.append(jnp.concatenate([
            jnp.where(low_half, a, pltpu.roll(b, LANES // 2, 1)),
            jnp.where(low_half, pltpu.roll(a, LANES // 2, 1), b)], axis=0))
    lhs = jnp.concatenate(lhs, axis=1).astype(BF16)
    downward = dot_nt(lhs, jnp.concatenate([weights[tile] for tile in range(n // 2)], axis=1)).astype(BF16)
    for q in range(leaves // 4):
        span = slice(q * 4 * m, (q + 1) * 4 * m)
        out_ref[:, span] = (base[:, span] + dot_nn(downward, response[:, span])).astype(BF16)

    take_all(all_send, 0)
    take_all(all_send, 1)
    for kind in range(3):
        halo_sent(kind)


def body(
    charges, leaf_basis, leaf_transfer, mid_transfer, far_source, far_coupling, mid_source, mid_coupling,
    box_coupling, top_transfer, top_coupling, near_target, near_source, near_count, near_blocks,
):
    n = lax.axis_size(AXIS)
    v, points = charges.shape
    leaves, k0 = far_source.shape
    m = points // leaves
    r0 = leaf_basis.shape[0]
    groups, k1 = mid_source.shape
    r = leaf_transfer.shape[1]
    capacity = near_target.shape[0]
    levels = (n // 4).bit_length() - 1
    tiles = sum((n >> level) // 2 + 1 for level in range(levels + 1))
    sizes = (v, leaves, m, r0, groups, r, k0, k1, capacity)
    vmem = pl.BlockSpec(memory_space=pltpu.VMEM)
    hbm = pl.BlockSpec(memory_space=pltpu.HBM)
    dma = pltpu.SemaphoreType.DMA
    return pl.pallas_call(
        functools.partial(kernel, n, sizes),
        out_shape=pltpu.VMEM(charges.shape, BF16),
        in_specs=[hbm] * 3 + [pl.BlockSpec(memory_space=pl.ANY)] + [hbm] * 11,
        out_specs=vmem,
        scratch_shapes=[
            pltpu.VMEM((3, v, points), BF16),
            pltpu.VMEM((3, v, leaves * r0), BF16),
            pltpu.VMEM((3, v, groups * r), BF16),
            pltpu.VMEM((n, v // 2, 2 * r), F32),
            pltpu.VMEM(leaf_basis.shape, BF16),
            pltpu.VMEM(leaf_transfer.shape, BF16),
            pltpu.VMEM(mid_transfer.shape[1:], BF16),
            pltpu.VMEM(far_coupling.shape, BF16),
            pltpu.VMEM(mid_coupling.shape, BF16),
            pltpu.VMEM(box_coupling.shape[1:], BF16),
            pltpu.VMEM(top_transfer.shape, BF16),
            pltpu.VMEM((levels,) + top_coupling.shape[1:], BF16),
            pltpu.VMEM(near_blocks.shape, BF16),
            pltpu.VMEM((capacity // LANES, LANES), jnp.int32),
            pltpu.VMEM((k0, leaves), jnp.int32),
            pltpu.VMEM((groups, k1), jnp.int32),
            pltpu.VMEM((capacity // LANES, LANES), jnp.int32),
            pltpu.SMEM((capacity // LANES, LANES), jnp.int32),
            pltpu.SMEM((k0, leaves), jnp.int32),
            pltpu.SMEM((groups, k1), jnp.int32),
            pltpu.VMEM((1, 1), jnp.int32),
            pltpu.VMEM((4 * leaves, v, LANES), F32),
            pltpu.VMEM((4 * leaves, v, LANES), F32),
            pltpu.VMEM((4 * groups, v, LANES), F32),
            pltpu.VMEM((capacity // 2 * v, 2 * m), F32),
            pltpu.VMEM((v, 2 * leaves, 2 * m), F32),
            pltpu.VMEM((v * leaves, 2 * m), F32),
            pltpu.VMEM((groups, v, leaves // groups * r0), F32),
            pltpu.VMEM((v, groups * r), F32),
            pltpu.VMEM((tiles, r, 2 * r), BF16),
            pltpu.VMEM((r, points), BF16),
            pltpu.VMEM((v, points), F32),
            pltpu.VMEM((capacity // LANES // 4, 2 * leaves, 2 * LANES), BF16),
            dma((13,)),
            dma((2 * CHUNKS,)),
            dma((levels,)),
            dma((3,)),
            dma((6,)),
            dma((6,)),
            dma((2,)),
            dma((2,)),
        ],
        compiler_params=pltpu.CompilerParams(
            collective_id=0, has_side_effects=True, vmem_limit_bytes=60 * 1024 * 1024),
    )(
        near_source.reshape(capacity // LANES, LANES), far_source.T, mid_source, near_count.reshape(1, 1), near_target.reshape(capacity // LANES, LANES),
        charges, leaf_basis, leaf_transfer, mid_transfer, far_coupling, mid_coupling,
        box_coupling, top_transfer, top_coupling, near_blocks,
    )


def solution(mesh):
    c = "clusters"
    in_specs = (
        P(None, c), P(None, c), P(c, None, None), P(c, None, None), P(c, None), P(c, None, None),
        P(c, None), P(c, None, None), P(c, None, None), P(), P(), P(c), P(c), P(c), P(None, c),
    )
    return jax.shard_map(body, mesh=mesh, in_specs=in_specs, out_specs=P(None, c), check_vma=False)
```

```python
import functools

import jax
import jax.numpy as jnp
from jax import lax
from jax.experimental import pallas as pl
from jax.experimental.pallas import tpu as pltpu
from jax.sharding import PartitionSpec as P

F32 = jnp.float32
BF16 = jnp.bfloat16
AXIS = "clusters"
NT = (((1,), (1,)), ((), ()))
NN = (((1,), (0,)), ((), ()))
LANES = 128
CHUNKS = 8
PASS_AT = 3


def dot_nt(a, b):
    return lax.dot_general(a, b, NT, preferred_element_type=F32)


def dot_nn(a, b):
    return lax.dot_general(a, b, NN, preferred_element_type=F32)


def lanes(shape):
    return lax.broadcasted_iota(jnp.int32, shape, len(shape) - 1)


def rows(shape):
    return lax.broadcasted_iota(jnp.int32, shape, len(shape) - 2)


def diagonal(out, v, width):
    blocks = out.shape[0] // v
    lane = lanes((v, out.shape[1])) // width
    total = jnp.zeros((v, out.shape[1]), F32)
    for block in range(blocks):
        total = jnp.where(lane == block, out[block * v:(block + 1) * v], total)
    return total


def kernel(
    n, sizes,
    near_source_h, far_source_h, mid_source_h, near_count_h, near_target_h,
    charges_h, basis_h, leaf_transfer_h, mid_transfer_h, far_coupling_h, mid_coupling_h,
    box_coupling_h, top_transfer_h, top_coupling_h, near_blocks_h,
    out_ref,
    cw, lw, mw, gathered, basis, leaf_transfer, mid_transfer, far_coupling, mid_coupling,
    box_coupling, top_transfer, top_coupling, near_blocks,
    near_raw, far_raw, mid_raw, near_target, near_source, far_source, mid_source, near_count,
    charge_tiles, leaf_tiles, mid_tiles, contribution, near_part, near_rows, leaf_far, mid_far, weights, response, base, masked_basis,
    assigned,
    load_sem, near_sem, top_sem, index_sem, halo_send, halo_recv, all_send, all_recv,
):
    v, leaves, m, r0, groups, r, k0, k1, capacity = sizes
    child = leaves // groups
    levels = (n // 4).bit_length() - 1
    across_layers = min(4, n)
    in_layer = n // across_layers
    me = lax.axis_index(AXIS)
    layer, place = me // in_layer, lax.rem(me, in_layer)
    half = lanes((v, LANES)) < m
    low_lane = lanes((v, LANES)) < r

    barrier = pltpu.get_barrier_semaphore()

    def above(step):
        return lax.rem(layer + step, across_layers) * in_layer + place

    def around(step):
        return layer * in_layer + lax.rem(place + step, in_layer)

    beside = jnp.where(place == 0, me - 1, me + 1)
    has_beside = ((place == 0) | (place == in_layer - 1)) & (beside >= 0) & (beside < n)

    def greet(other):
        pl.semaphore_signal(barrier, inc=1, device_id=(other,), device_id_type=pl.DeviceIdType.MESH)

    for step in range(1, across_layers):
        greet(above(step))

    def greet_around(step, carry):
        greet(around(step))
        return carry

    lax.fori_loop(1, in_layer, greet_around, 0)

    @pl.when(has_beside)
    def _():
        greet(beside)

    pairs = [
        (charges_h, cw.at[1]), (basis_h, basis), (leaf_transfer_h, leaf_transfer), (mid_transfer_h.at[0], mid_transfer),
        (mid_coupling_h, mid_coupling), (far_coupling_h, far_coupling), (box_coupling_h.at[0], box_coupling),
        (top_transfer_h, top_transfer), (near_source_h, near_raw), (far_source_h, far_raw), (mid_source_h, mid_raw),
        (near_target_h, near_target), (near_count_h, near_count),
    ]
    loads = [pltpu.make_async_copy(s, d, load_sem.at[i]) for i, (s, d) in enumerate(pairs)]
    side = capacity // 2
    width = side * m // CHUNKS

    def near_load(chunk, part):
        span = pl.ds(part * side * m + chunk * width, width)
        return pltpu.make_async_copy(
            near_blocks_h.at[:, span], near_blocks.at[:, span], near_sem.at[2 * chunk + part])

    tops = []
    for level in range(1, levels + 1):
        start = n - (n >> (level - 1))
        tops.append(pltpu.make_async_copy(
            top_coupling_h.at[start + (me >> level)], top_coupling.at[level - 1], top_sem.at[level - 1]))

    for i in (0, 1, 2, 3, 8, 9, 10, 11, 12, 6, 7):
        loads[i].start()
    for copy in tops:
        copy.start()
    loads[5].start()
    for chunk in range(CHUNKS):
        near_load(chunk, 0).start()
        near_load(chunk, 1).start()
    loads[4].start()

    loads[0].wait()
    loads[1].wait()
    span_points = child * m
    lane_leaf = lanes((v, span_points)) // m
    ups = []
    for c in range(groups):
        x = cw[1, :, c * span_points:(c + 1) * span_points].astype(F32)
        lhs = jnp.concatenate([jnp.where(lane_leaf == l, x, 0.0) for l in range(child)], axis=0).astype(BF16)
        b = basis[:, c * span_points:(c + 1) * span_points]
        up = diagonal(dot_nt(lhs, jnp.concatenate([b] * child, axis=0)), v, r0).astype(BF16)
        lw[1, :, c * child * r0:(c + 1) * child * r0] = up
        ups.append(up.astype(F32))
    loads[2].wait()
    loads[3].wait()
    quad = 4
    for g in range(groups // quad):
        lhs = jnp.concatenate(ups[g * quad:(g + 1) * quad], axis=0).astype(BF16)
        matrix = leaf_transfer[g * quad:(g + 1) * quad].reshape(quad * r, child * r0)
        mw[1, :, g * quad * r:(g + 1) * quad * r] = diagonal(dot_nt(lhs, matrix), v, r).astype(BF16)
    transfer = mid_transfer[...]
    box_up = dot_nt(mw[1], jnp.concatenate([transfer, transfer], axis=0))
    gathered[place * across_layers + layer] = jnp.where(low_lane[:v // 2], box_up[:v // 2], box_up[v // 2:])

    wides = (cw, lw, mw)

    def halo(kind, side):
        wide = wides[kind]
        return pltpu.make_async_remote_copy(
            src_ref=wide.at[1], dst_ref=wide.at[2 - 2 * side], send_sem=halo_send.at[2 * kind + side],
            recv_sem=halo_recv.at[2 * kind + side], device_id=(me - 1 + 2 * side,),
            device_id_type=pl.DeviceIdType.MESH)

    def halo_starts(kind):
        @pl.when(me > 0)
        def _():
            halo(kind, 0).start()

        @pl.when(me < n - 1)
        def _():
            halo(kind, 1).start()

    def halo_arrive(kind):
        wide = wides[kind]

        @pl.when(me < n - 1)
        def _():
            halo(kind, 0).wait_recv()

        @pl.when(me > 0)
        def _():
            halo(kind, 1).wait_recv()

        @pl.when(me == 0)
        def _():
            wide[0] = jnp.zeros(wide.shape[1:], BF16)

        @pl.when(me == n - 1)
        def _():
            wide[2] = jnp.zeros(wide.shape[1:], BF16)

    def halo_sent(kind):
        @pl.when(me > 0)
        def _():
            halo(kind, 0).wait_send()

        @pl.when(me < n - 1)
        def _():
            halo(kind, 1).wait_send()

    def rise(step):
        own = gathered.at[place * across_layers + layer]
        return pltpu.make_async_remote_copy(
            src_ref=own, dst_ref=own, send_sem=all_send.at[0], recv_sem=all_recv.at[0],
            device_id=(above(step),), device_id_type=pl.DeviceIdType.MESH)

    def share(step):
        own = gathered.at[pl.ds(place * across_layers, across_layers)]
        return pltpu.make_async_remote_copy(
            src_ref=own, dst_ref=own, send_sem=all_send.at[1], recv_sem=all_recv.at[1],
            device_id=(around(step),), device_id_type=pl.DeviceIdType.MESH)

    def share_step(step, carry):
        share(step).start()
        return carry

    def take_all(sems, stage):
        count = (across_layers - 1, (in_layer - 1) * across_layers)[stage]
        block = gathered.at[pl.ds(0, count)]
        pltpu.make_async_copy(block, block, sems.at[stage]).wait()

    def pass_on():
        take_all(all_recv, 0)
        lax.fori_loop(1, in_layer, share_step, 0)

    pl.semaphore_wait(barrier, across_layers + in_layer - 2 + has_beside.astype(jnp.int32))

    for step in range(1, across_layers):
        rise(step).start()
    halo_starts(1)
    halo_starts(0)
    halo_starts(2)

    for i in (8, 9, 10):
        loads[i].wait()
    near_raw[...] = near_raw[...] & (4 * leaves - 1)
    far_raw[...] = far_raw[...] & (4 * leaves - 1)
    mid_raw[...] = mid_raw[...] & (4 * groups - 1)
    index_copies = [pltpu.make_async_copy(a, b, index_sem.at[i]) for i, (a, b) in enumerate(
        ((near_raw, near_source), (far_raw, far_source), (mid_raw, mid_source)))]
    for copy in index_copies:
        copy.start()

    loads[11].wait()
    loads[12].wait()
    count = near_count[...]
    leaf_row = rows((leaves, LANES))
    slot_lane = lanes((leaves, LANES))
    assignment = []
    for b in range(capacity // LANES):
        hit = (leaf_row == near_target[b:b + 1, :]) & (slot_lane + b * LANES < count)
        assignment.append(jnp.where(hit, 1.0, 0.0).astype(BF16))
    strips = side // LANES
    for b in range(strips // 2):
        low = jnp.concatenate(assignment[2 * b:2 * b + 2], axis=1)
        high = jnp.concatenate(assignment[strips + 2 * b:strips + 2 * b + 2], axis=1)
        assigned[b] = jnp.concatenate([low, high], axis=0)
    def put(tiles, slot, value):
        tiles[slot] = value

    def take(tiles, slot):
        return tiles[slot]

    def spread_pairs(wide, tiles, per_box, box):
        x = wide[box].astype(F32)
        first = lax.rem(me + 3 + box, 4) * per_box
        for t in range(per_box // 2):
            tile = x[:, t * LANES:(t + 1) * LANES]
            turned = pltpu.roll(tile, LANES // 2, 1)
            put(tiles, first + 2 * t, jnp.where(half, tile, turned))
            put(tiles, first + 2 * t + 1, jnp.where(half, turned, tile))

    fold = LANES // r0
    lane_block = lanes((v, LANES)) // r0

    def spread_leaves(box):
        x = lw[box].astype(F32)
        first = lax.rem(me + 3 + box, 4) * leaves
        for t in range(leaves // fold):
            tile = x[:, t * LANES:(t + 1) * LANES]
            turned = [tile] + [pltpu.roll(tile, r0 * k, 1) for k in range(1, fold)]
            for p in range(fold):
                piece = turned[(0 - p) % fold]
                for w in range(1, fold):
                    piece = jnp.where(lane_block == w, turned[(w - p) % fold], piece)
                put(leaf_tiles, first + t * fold + p, piece)

    for tiles, per_box in ((charge_tiles, leaves), (leaf_tiles, leaves), (mid_tiles, groups)):
        unused = pl.ds(lax.rem(me + 2, 4) * per_box, per_box)
        tiles[unused] = jnp.zeros((per_box, v, LANES), F32)
    spread_pairs(cw, charge_tiles, leaves, 1)
    spread_leaves(1)
    spread_pairs(mw, mid_tiles, groups, 1)

    loads[6].wait()
    loads[7].wait()
    for copy in tops:
        copy.wait()
    offsets = []
    offset = 0
    for level in range(levels + 1):
        offsets.append(offset)
        offset += (n >> level) // 2 + 1
    wide_low = lanes((r, LANES)) < r
    diagonal_lane = lanes((r, LANES)) - rows((r, LANES))
    chain = None
    pushed = []
    for level in range(levels + 1):
        cluster = me >> level
        odd = lax.rem(cluster, 2)
        if level == 0:
            q = box_coupling[...].astype(F32)
        else:
            q = dot_nn(chain[:, :r].astype(BF16), top_coupling[level - 1])
        pair = q[:, :LANES]
        turned = pltpu.roll(pair, LANES // 2, 1)
        third = jnp.concatenate([q[:, LANES:], q[:, LANES:]], axis=1)
        is_odd = odd.astype(F32)
        before = jnp.where(wide_low, pair, pair * is_odd)
        after = jnp.where(wide_low, turned * (1.0 - is_odd), third)
        pushed.append((before.astype(BF16), after.astype(BF16)))
        if level < levels:
            t = top_transfer[n - (n >> level) + (cluster >> 1)]
            t = jnp.concatenate([t, t], axis=0)
            if level == 0:
                lhs = jnp.where(diagonal_lane == r * odd, 1.0, 0.0)
            else:
                lhs = jnp.where(wide_low, chain * (1.0 - is_odd), chain * is_odd)
            chain = dot_nt(lhs.astype(BF16), t)
    blank = jnp.zeros((r, LANES), BF16)
    for level in range(levels, -1, -1):
        tiles = (n >> level) // 2
        if level == levels:
            for tile in range(tiles):
                weights[offsets[level] + tile] = blank
        else:
            above = n - (n >> level)
            for tile in range(tiles // 2):
                zero_block = jnp.zeros((r, 2 * r), BF16)
                matrix = jnp.concatenate([
                    jnp.concatenate([top_transfer[above + 2 * tile], zero_block], axis=1),
                    jnp.concatenate([zero_block, top_transfer[above + 2 * tile + 1]], axis=1)], axis=0)
                out = dot_nn(weights[offsets[level + 1] + tile], matrix).astype(BF16)
                weights[offsets[level] + 2 * tile] = out[:, :LANES]
                weights[offsets[level] + 2 * tile + 1] = out[:, LANES:]
        own = me >> (level + 1)
        weights[offsets[level] + jnp.where(own > 0, own - 1, tiles)] = pushed[level][0]
        weights[offsets[level] + jnp.where(own + 1 < tiles, own + 1, tiles)] = pushed[level][1]

    quad_mask = (rows((4 * r0, 4 * m)) // r0 == lanes((4 * r0, 4 * m)) // m).astype(F32).astype(BF16)
    for pair in range(groups // 2):
        tile = mid_transfer[:, pair * LANES:(pair + 1) * LANES].astype(F32)
        lhs = jnp.concatenate([jnp.where(wide_low, tile, 0.0), jnp.where(wide_low, 0.0, tile)], axis=0).astype(BF16)
        push = dot_nn(lhs, leaf_transfer[2 * pair:2 * pair + 2].reshape(2 * r, child * r0)).astype(BF16)
        for s in range(2):
            for h in range(child // 4):
                q = (2 * pair + s) * (child // 4) + h
                b = jnp.concatenate([basis[:, q * 4 * m:(q + 1) * 4 * m]] * 4, axis=0) * quad_mask
                masked_basis[q] = b
                lhs = push[s * r:(s + 1) * r, h * 4 * r0:(h + 1) * 4 * r0]
                response[:, q * 4 * m:(q + 1) * 4 * m] = dot_nn(lhs, b).astype(BF16)

    for copy in index_copies:
        copy.wait()
    halo_arrive(1)
    spread_leaves(0)
    spread_leaves(2)
    loads[5].wait()

    def far_step(c, carry):
        parts = []
        for l in range(child):
            tiles = []
            for t in range(k0 // fold):
                piece = take(leaf_tiles, far_source[t * fold, c * child + l])
                for w in range(1, fold):
                    piece = jnp.where(lane_block == w, take(leaf_tiles, far_source[t * fold + w, c * child + l]), piece)
                tiles.append(piece)
            parts.append(jnp.concatenate(tiles, axis=1))
        lhs = jnp.concatenate(parts, axis=0).astype(BF16)
        matrix = far_coupling[c * child:(c + 1) * child].reshape(child * r0, k0 * r0)
        leaf_far[c] = diagonal(dot_nt(lhs, matrix), v, r0)
        return carry


    halo_arrive(0)
    halo_arrive(2)
    spread_pairs(mw, mid_tiles, groups, 0)
    spread_pairs(mw, mid_tiles, groups, 2)
    loads[4].wait()
    for g in range(groups // quad):
        parts = []
        for c in range(g * quad, (g + 1) * quad):
            tiles = []
            for t in range(k1 // 2):
                a = take(mid_tiles, mid_source[c, 2 * t])
                b = take(mid_tiles, mid_source[c, 2 * t + 1])
                tiles.append(jnp.where(half, a, b))
            parts.append(jnp.concatenate(tiles, axis=1))
        lhs = jnp.concatenate(parts, axis=0).astype(BF16)
        matrix = mid_coupling[g * quad:(g + 1) * quad].reshape(quad * r, k1 * r)
        mid_far[:, g * quad * r:(g + 1) * quad * r] = diagonal(dot_nt(lhs, matrix), v, r)

    def base_step(pair):
        tile = mid_far[:, pair * LANES:(pair + 1) * LANES]
        lhs = jnp.concatenate([jnp.where(low_lane, tile, 0.0), jnp.where(low_lane, 0.0, tile)], axis=0).astype(BF16)
        push = dot_nn(lhs, leaf_transfer[2 * pair:2 * pair + 2].reshape(2 * r, child * r0))
        for s in range(2):
            c = 2 * pair + s
            lhs = (leaf_far[c] + push[s * v:(s + 1) * v]).astype(BF16)
            for h in range(child // 4):
                q = c * (child // 4) + h
                base[:, q * 4 * m:(q + 1) * 4 * m] = dot_nn(lhs[:, h * 4 * r0:(h + 1) * 4 * r0], masked_basis[q])

    spread_pairs(cw, charge_tiles, leaves, 0)
    spread_pairs(cw, charge_tiles, leaves, 2)

    zero = jnp.zeros((2 * v, LANES), F32)

    def gather(first):
        pieces = []
        for i in range(4):
            slot = first + i
            x = take(charge_tiles, near_source[slot // LANES, slot % LANES])
            pieces.append(jnp.where(half, x, 0.0) if i % 2 == 0 else jnp.where(half, 0.0, x))
        upper = jnp.concatenate([pieces[0], pieces[1]], axis=0)
        lower = jnp.concatenate([pieces[2], pieces[3]], axis=0)
        return jnp.concatenate(
            [jnp.concatenate([upper, zero], axis=1), jnp.concatenate([zero, lower], axis=1)], axis=0).astype(BF16)

    def collect(b, u):
        c = contribution[pl.ds(b * 2 * LANES * v + u, 2 * LANES, stride=v), :]
        return dot_nn(assigned[b], c.astype(BF16))

    steps = side // 4
    spans = side // (2 * LANES)
    per_span = steps // spans
    every = per_span // v
    wide_half = lanes((leaves, LANES)) < m
    mixed_half = lanes((4 * v, LANES)) < m
    for g in range(steps):
        if g == PASS_AT * steps // 8:
            pass_on()
        if g % (steps // CHUNKS) == 0:
            near_load(g // (steps // CHUNKS), 0).wait()
            near_load(g // (steps // CHUNKS), 1).wait()
        lhs = jnp.concatenate([gather(g * 4), gather(side + g * 4)], axis=0)
        block = jnp.concatenate([
            near_blocks[:, g * 4 * m:(g + 1) * 4 * m],
            near_blocks[:, (side + g * 4) * m:(side + (g + 1) * 4) * m]], axis=0)
        out = dot_nt(lhs, block)
        contribution[g * 4 * v:(g + 1) * 4 * v, :] = jnp.where(mixed_half, out[:4 * v], out[4 * v:])
        if g * groups % steps == 0:
            c = g * groups // steps
            far_step(c, 0)
            if c % 2 == 1:
                base_step(c // 2)
        span = g // per_span
        if span > 0 and g % every == every - 1:
            u = g % per_span // every
            part = collect(span - 1, u)
            near_part[u] = part if span == 1 else near_part[u] + part

    for u in range(v):
        total = collect(spans - 1, u)
        if spans > 1:
            total = total + near_part[u]
        mixed = jnp.where(wide_half, total[:leaves], total[leaves:])
        near_rows[u * leaves:(u + 1) * leaves, :] = mixed + pltpu.roll(mixed, LANES // 2, 1)

    for q in range(leaves // 4):
        for w in range(2):
            leaf = q * 4 + 2 * w
            even = near_rows[pl.ds(leaf, v, stride=leaves), :]
            odd = near_rows[pl.ds(leaf + 1, v, stride=leaves), :]
            base[:, leaf * m:(leaf + 2) * m] += jnp.where(half, even, odd)

    take_all(all_recv, 1)

    def box(b):
        return gathered[b % in_layer * across_layers + b // in_layer]

    low_half = low_lane[:v // 2]
    lhs = []
    for tile in range(n // 2):
        a = box(2 * tile)
        b = box(2 * tile + 1)
        lhs.append(jnp.concatenate([
            jnp.where(low_half, a, pltpu.roll(b, LANES // 2, 1)),
            jnp.where(low_half, pltpu.roll(a, LANES // 2, 1), b)], axis=0))
    lhs = jnp.concatenate(lhs, axis=1).astype(BF16)
    downward = dot_nt(lhs, jnp.concatenate([weights[tile] for tile in range(n // 2)], axis=1)).astype(BF16)
    for q in range(leaves // 4):
        span = slice(q * 4 * m, (q + 1) * 4 * m)
        out_ref[:, span] = (base[:, span] + dot_nn(downward, response[:, span])).astype(BF16)

    take_all(all_send, 0)
    take_all(all_send, 1)
    for kind in range(3):
        halo_sent(kind)


def body(
    charges, leaf_basis, leaf_transfer, mid_transfer, far_source, far_coupling, mid_source, mid_coupling,
    box_coupling, top_transfer, top_coupling, near_target, near_source, near_count, near_blocks,
):
    n = lax.axis_size(AXIS)
    v, points = charges.shape
    leaves, k0 = far_source.shape
    m = points // leaves
    r0 = leaf_basis.shape[0]
    groups, k1 = mid_source.shape
    r = leaf_transfer.shape[1]
    capacity = near_target.shape[0]
    levels = (n // 4).bit_length() - 1
    tiles = sum((n >> level) // 2 + 1 for level in range(levels + 1))
    sizes = (v, leaves, m, r0, groups, r, k0, k1, capacity)
    vmem = pl.BlockSpec(memory_space=pltpu.VMEM)
    hbm = pl.BlockSpec(memory_space=pltpu.HBM)
    dma = pltpu.SemaphoreType.DMA
    return pl.pallas_call(
        functools.partial(kernel, n, sizes),
        out_shape=pltpu.VMEM(charges.shape, BF16),
        in_specs=[hbm] * 3 + [pl.BlockSpec(memory_space=pl.ANY)] + [hbm] * 11,
        out_specs=vmem,
        scratch_shapes=[
            pltpu.VMEM((3, v, points), BF16),
            pltpu.VMEM((3, v, leaves * r0), BF16),
            pltpu.VMEM((3, v, groups * r), BF16),
            pltpu.VMEM((n, v // 2, 2 * r), F32),
            pltpu.VMEM(leaf_basis.shape, BF16),
            pltpu.VMEM(leaf_transfer.shape, BF16),
            pltpu.VMEM(mid_transfer.shape[1:], BF16),
            pltpu.VMEM(far_coupling.shape, BF16),
            pltpu.VMEM(mid_coupling.shape, BF16),
            pltpu.VMEM(box_coupling.shape[1:], BF16),
            pltpu.VMEM(top_transfer.shape, BF16),
            pltpu.VMEM((levels,) + top_coupling.shape[1:], BF16),
            pltpu.VMEM(near_blocks.shape, BF16),
            pltpu.VMEM((capacity // LANES, LANES), jnp.int32),
            pltpu.VMEM((k0, leaves), jnp.int32),
            pltpu.VMEM((groups, k1), jnp.int32),
            pltpu.VMEM((capacity // LANES, LANES), jnp.int32),
            pltpu.SMEM((capacity // LANES, LANES), jnp.int32),
            pltpu.SMEM((k0, leaves), jnp.int32),
            pltpu.SMEM((groups, k1), jnp.int32),
            pltpu.VMEM((1, 1), jnp.int32),
            pltpu.VMEM((4 * leaves, v, LANES), F32),
            pltpu.VMEM((4 * leaves, v, LANES), F32),
            pltpu.VMEM((4 * groups, v, LANES), F32),
            pltpu.VMEM((capacity // 2 * v, 2 * m), F32),
            pltpu.VMEM((v, 2 * leaves, 2 * m), F32),
            pltpu.VMEM((v * leaves, 2 * m), F32),
            pltpu.VMEM((groups, v, leaves // groups * r0), F32),
            pltpu.VMEM((v, groups * r), F32),
            pltpu.VMEM((tiles, r, 2 * r), BF16),
            pltpu.VMEM((r, points), BF16),
            pltpu.VMEM((v, points), F32),
            pltpu.VMEM((leaves // 4, 4 * r0, 4 * m), BF16),
            pltpu.VMEM((capacity // LANES // 4, 2 * leaves, 2 * LANES), BF16),
            dma((13,)),
            dma((2 * CHUNKS,)),
            dma((levels,)),
            dma((3,)),
            dma((6,)),
            dma((6,)),
            dma((2,)),
            dma((2,)),
        ],
        compiler_params=pltpu.CompilerParams(
            collective_id=0, has_side_effects=True, vmem_limit_bytes=60 * 1024 * 1024),
    )(
        near_source.reshape(capacity // LANES, LANES), far_source.T, mid_source, near_count.reshape(1, 1), near_target.reshape(capacity // LANES, LANES),
        charges, leaf_basis, leaf_transfer, mid_transfer, far_coupling, mid_coupling,
        box_coupling, top_transfer, top_coupling, near_blocks,
    )


def solution(mesh):
    c = "clusters"
    in_specs = (
        P(None, c), P(None, c), P(c, None, None), P(c, None, None), P(c, None), P(c, None, None),
        P(c, None), P(c, None, None), P(c, None, None), P(), P(), P(c), P(c), P(c), P(None, c),
    )
    return jax.shard_map(body, mesh=mesh, in_specs=in_specs, out_specs=P(None, c), check_vma=False)
```

```python
import functools

import jax
import jax.numpy as jnp
from jax import lax
from jax.experimental import pallas as pl
from jax.experimental.pallas import tpu as pltpu
from jax.sharding import PartitionSpec as P

F32 = jnp.float32
BF16 = jnp.bfloat16
AXIS = "clusters"
NT = (((1,), (1,)), ((), ()))
NN = (((1,), (0,)), ((), ()))
LANES = 128
CHUNKS = 4
PASS_AT = 2


def dot_nt(a, b):
    return lax.dot_general(a, b, NT, preferred_element_type=F32)


def dot_nn(a, b):
    return lax.dot_general(a, b, NN, preferred_element_type=F32)


def lanes(shape):
    return lax.broadcasted_iota(jnp.int32, shape, len(shape) - 1)


def rows(shape):
    return lax.broadcasted_iota(jnp.int32, shape, len(shape) - 2)


def diagonal(out, v, width):
    blocks = out.shape[0] // v
    lane = lanes((v, out.shape[1])) // width
    total = jnp.zeros((v, out.shape[1]), F32)
    for block in range(blocks):
        total = jnp.where(lane == block, out[block * v:(block + 1) * v], total)
    return total


def kernel(
    n, sizes,
    near_source_h, far_source_h, mid_source_h, near_count_h, near_target_h,
    charges_h, basis_h, leaf_transfer_h, mid_transfer_h, far_coupling_h, mid_coupling_h,
    box_coupling_h, top_transfer_h, top_coupling_h, near_blocks_h,
    out_ref,
    cw, lw, mw, gathered, basis, leaf_transfer, mid_transfer, far_coupling, mid_coupling,
    box_coupling, top_transfer, top_coupling, near_blocks,
    near_raw, far_raw, mid_raw, near_target, near_source, far_source, mid_source, near_count,
    charge_tiles, leaf_tiles, mid_tiles, contribution, near_part, near_rows, leaf_far, mid_far, weights, response, base, masked_basis,
    assigned,
    load_sem, near_sem, top_sem, index_sem, halo_send, halo_recv, all_send, all_recv,
):
    v, leaves, m, r0, groups, r, k0, k1, capacity = sizes
    child = leaves // groups
    levels = (n // 4).bit_length() - 1
    across_layers = min(4, n)
    in_layer = n // across_layers
    me = lax.axis_index(AXIS)
    layer, place = me // in_layer, lax.rem(me, in_layer)
    half = lanes((v, LANES)) < m
    low_lane = lanes((v, LANES)) < r

    barrier = pltpu.get_barrier_semaphore()

    def above(step):
        return lax.rem(layer + step, across_layers) * in_layer + place

    def around(step):
        return layer * in_layer + lax.rem(place + step, in_layer)

    beside = jnp.where(place == 0, me - 1, me + 1)
    has_beside = ((place == 0) | (place == in_layer - 1)) & (beside >= 0) & (beside < n)

    def greet(other):
        pl.semaphore_signal(barrier, inc=1, device_id=(other,), device_id_type=pl.DeviceIdType.MESH)

    for step in range(1, across_layers):
        greet(above(step))

    def greet_around(step, carry):
        greet(around(step))
        return carry

    lax.fori_loop(1, in_layer, greet_around, 0)

    @pl.when(has_beside)
    def _():
        greet(beside)

    pairs = [
        (charges_h, cw.at[1]), (basis_h, basis), (leaf_transfer_h, leaf_transfer), (mid_transfer_h.at[0], mid_transfer),
        (mid_coupling_h, mid_coupling), (far_coupling_h, far_coupling), (box_coupling_h.at[0], box_coupling),
        (top_transfer_h, top_transfer), (near_source_h, near_raw), (far_source_h, far_raw), (mid_source_h, mid_raw),
        (near_target_h, near_target), (near_count_h, near_count),
    ]
    loads = [pltpu.make_async_copy(s, d, load_sem.at[i]) for i, (s, d) in enumerate(pairs)]
    side = capacity // 2
    width = side * m // CHUNKS

    def near_load(chunk, part):
        span = pl.ds(part * side * m + chunk * width, width)
        return pltpu.make_async_copy(
            near_blocks_h.at[:, span], near_blocks.at[:, span], near_sem.at[2 * chunk + part])

    tops = []
    for level in range(1, levels + 1):
        start = n - (n >> (level - 1))
        tops.append(pltpu.make_async_copy(
            top_coupling_h.at[start + (me >> level)], top_coupling.at[level - 1], top_sem.at[level - 1]))

    for i in (0, 1, 2, 3, 8, 9, 10, 11, 12, 6, 7):
        loads[i].start()
    for copy in tops:
        copy.start()
    loads[5].start()
    for chunk in range(CHUNKS):
        near_load(chunk, 0).start()
        near_load(chunk, 1).start()
    loads[4].start()

    loads[0].wait()
    loads[1].wait()
    span_points = child * m
    lane_leaf = lanes((v, span_points)) // m
    ups = []
    for c in range(groups):
        x = cw[1, :, c * span_points:(c + 1) * span_points].astype(F32)
        lhs = jnp.concatenate([jnp.where(lane_leaf == l, x, 0.0) for l in range(child)], axis=0).astype(BF16)
        b = basis[:, c * span_points:(c + 1) * span_points]
        up = diagonal(dot_nt(lhs, jnp.concatenate([b] * child, axis=0)), v, r0).astype(BF16)
        lw[1, :, c * child * r0:(c + 1) * child * r0] = up
        ups.append(up.astype(F32))
    loads[2].wait()
    loads[3].wait()
    quad = 4
    for g in range(groups // quad):
        lhs = jnp.concatenate(ups[g * quad:(g + 1) * quad], axis=0).astype(BF16)
        matrix = leaf_transfer[g * quad:(g + 1) * quad].reshape(quad * r, child * r0)
        mw[1, :, g * quad * r:(g + 1) * quad * r] = diagonal(dot_nt(lhs, matrix), v, r).astype(BF16)
    transfer = mid_transfer[...]
    box_up = dot_nt(mw[1], jnp.concatenate([transfer, transfer], axis=0))
    gathered[place * across_layers + layer] = jnp.where(low_lane[:v // 2], box_up[:v // 2], box_up[v // 2:])

    wides = (cw, lw, mw)

    def halo(kind, side):
        wide = wides[kind]
        return pltpu.make_async_remote_copy(
            src_ref=wide.at[1], dst_ref=wide.at[2 - 2 * side], send_sem=halo_send.at[2 * kind + side],
            recv_sem=halo_recv.at[2 * kind + side], device_id=(me - 1 + 2 * side,),
            device_id_type=pl.DeviceIdType.MESH)

    def halo_starts(kind):
        @pl.when(me > 0)
        def _():
            halo(kind, 0).start()

        @pl.when(me < n - 1)
        def _():
            halo(kind, 1).start()

    def halo_arrive(kind):
        wide = wides[kind]

        @pl.when(me < n - 1)
        def _():
            halo(kind, 0).wait_recv()

        @pl.when(me > 0)
        def _():
            halo(kind, 1).wait_recv()

        @pl.when(me == 0)
        def _():
            wide[0] = jnp.zeros(wide.shape[1:], BF16)

        @pl.when(me == n - 1)
        def _():
            wide[2] = jnp.zeros(wide.shape[1:], BF16)

    def halo_sent(kind):
        @pl.when(me > 0)
        def _():
            halo(kind, 0).wait_send()

        @pl.when(me < n - 1)
        def _():
            halo(kind, 1).wait_send()

    def rise(step):
        own = gathered.at[place * across_layers + layer]
        return pltpu.make_async_remote_copy(
            src_ref=own, dst_ref=own, send_sem=all_send.at[0], recv_sem=all_recv.at[0],
            device_id=(above(step),), device_id_type=pl.DeviceIdType.MESH)

    def share(step):
        own = gathered.at[pl.ds(place * across_layers, across_layers)]
        return pltpu.make_async_remote_copy(
            src_ref=own, dst_ref=own, send_sem=all_send.at[1], recv_sem=all_recv.at[1],
            device_id=(around(step),), device_id_type=pl.DeviceIdType.MESH)

    def share_step(step, carry):
        share(step).start()
        return carry

    def take_all(sems, stage):
        count = (across_layers - 1, (in_layer - 1) * across_layers)[stage]
        block = gathered.at[pl.ds(0, count)]
        pltpu.make_async_copy(block, block, sems.at[stage]).wait()

    def pass_on():
        take_all(all_recv, 0)
        lax.fori_loop(1, in_layer, share_step, 0)

    pl.semaphore_wait(barrier, across_layers + in_layer - 2 + has_beside.astype(jnp.int32))

    for step in range(1, across_layers):
        rise(step).start()
    halo_starts(1)
    halo_starts(0)
    halo_starts(2)

    for i in (8, 9, 10):
        loads[i].wait()
    near_raw[...] = near_raw[...] & (4 * leaves - 1)
    far_raw[...] = far_raw[...] & (4 * leaves - 1)
    mid_raw[...] = mid_raw[...] & (4 * groups - 1)
    index_copies = [pltpu.make_async_copy(a, b, index_sem.at[i]) for i, (a, b) in enumerate(
        ((near_raw, near_source), (far_raw, far_source), (mid_raw, mid_source)))]
    for copy in index_copies:
        copy.start()

    loads[11].wait()
    loads[12].wait()
    count = near_count[...]
    leaf_row = rows((leaves, LANES))
    slot_lane = lanes((leaves, LANES))
    assignment = []
    for b in range(capacity // LANES):
        hit = (leaf_row == near_target[b:b + 1, :]) & (slot_lane + b * LANES < count)
        assignment.append(jnp.where(hit, 1.0, 0.0).astype(BF16))
    strips = side // LANES
    for b in range(strips // 2):
        low = jnp.concatenate(assignment[2 * b:2 * b + 2], axis=1)
        high = jnp.concatenate(assignment[strips + 2 * b:strips + 2 * b + 2], axis=1)
        assigned[b] = jnp.concatenate([low, high], axis=0)
    def put(tiles, slot, value):
        tiles[slot] = value

    def take(tiles, slot):
        return tiles[slot]

    def spread_pairs(wide, tiles, per_box, box):
        x = wide[box].astype(F32)
        first = lax.rem(me + 3 + box, 4) * per_box
        for t in range(per_box // 2):
            tile = x[:, t * LANES:(t + 1) * LANES]
            turned = pltpu.roll(tile, LANES // 2, 1)
            put(tiles, first + 2 * t, jnp.where(half, tile, turned))
            put(tiles, first + 2 * t + 1, jnp.where(half, turned, tile))

    fold = LANES // r0
    lane_block = lanes((v, LANES)) // r0

    def spread_leaves(box):
        x = lw[box].astype(F32)
        first = lax.rem(me + 3 + box, 4) * leaves
        for t in range(leaves // fold):
            tile = x[:, t * LANES:(t + 1) * LANES]
            turned = [tile] + [pltpu.roll(tile, r0 * k, 1) for k in range(1, fold)]
            for p in range(fold):
                piece = turned[(0 - p) % fold]
                for w in range(1, fold):
                    piece = jnp.where(lane_block == w, turned[(w - p) % fold], piece)
                put(leaf_tiles, first + t * fold + p, piece)

    for tiles, per_box in ((charge_tiles, leaves), (leaf_tiles, leaves), (mid_tiles, groups)):
        unused = pl.ds(lax.rem(me + 2, 4) * per_box, per_box)
        tiles[unused] = jnp.zeros((per_box, v, LANES), F32)
    spread_pairs(cw, charge_tiles, leaves, 1)
    spread_leaves(1)
    spread_pairs(mw, mid_tiles, groups, 1)

    loads[6].wait()
    loads[7].wait()
    for copy in tops:
        copy.wait()
    offsets = []
    offset = 0
    for level in range(levels + 1):
        offsets.append(offset)
        offset += (n >> level) // 2 + 1
    wide_low = lanes((r, LANES)) < r
    diagonal_lane = lanes((r, LANES)) - rows((r, LANES))
    chain = None
    pushed = []
    for level in range(levels + 1):
        cluster = me >> level
        odd = lax.rem(cluster, 2)
        if level == 0:
            q = box_coupling[...].astype(F32)
        else:
            q = dot_nn(chain[:, :r].astype(BF16), top_coupling[level - 1])
        pair = q[:, :LANES]
        turned = pltpu.roll(pair, LANES // 2, 1)
        third = jnp.concatenate([q[:, LANES:], q[:, LANES:]], axis=1)
        is_odd = odd.astype(F32)
        before = jnp.where(wide_low, pair, pair * is_odd)
        after = jnp.where(wide_low, turned * (1.0 - is_odd), third)
        pushed.append((before.astype(BF16), after.astype(BF16)))
        if level < levels:
            t = top_transfer[n - (n >> level) + (cluster >> 1)]
            t = jnp.concatenate([t, t], axis=0)
            if level == 0:
                lhs = jnp.where(diagonal_lane == r * odd, 1.0, 0.0)
            else:
                lhs = jnp.where(wide_low, chain * (1.0 - is_odd), chain * is_odd)
            chain = dot_nt(lhs.astype(BF16), t)
    blank = jnp.zeros((r, LANES), BF16)
    for level in range(levels, -1, -1):
        tiles = (n >> level) // 2
        if level == levels:
            for tile in range(tiles):
                weights[offsets[level] + tile] = blank
        else:
            above = n - (n >> level)
            for tile in range(tiles // 2):
                zero_block = jnp.zeros((r, 2 * r), BF16)
                matrix = jnp.concatenate([
                    jnp.concatenate([top_transfer[above + 2 * tile], zero_block], axis=1),
                    jnp.concatenate([zero_block, top_transfer[above + 2 * tile + 1]], axis=1)], axis=0)
                out = dot_nn(weights[offsets[level + 1] + tile], matrix).astype(BF16)
                weights[offsets[level] + 2 * tile] = out[:, :LANES]
                weights[offsets[level] + 2 * tile + 1] = out[:, LANES:]
        own = me >> (level + 1)
        weights[offsets[level] + jnp.where(own > 0, own - 1, tiles)] = pushed[level][0]
        weights[offsets[level] + jnp.where(own + 1 < tiles, own + 1, tiles)] = pushed[level][1]

    quad_mask = (rows((4 * r0, 4 * m)) // r0 == lanes((4 * r0, 4 * m)) // m).astype(F32).astype(BF16)
    for pair in range(groups // 2):
        tile = mid_transfer[:, pair * LANES:(pair + 1) * LANES].astype(F32)
        lhs = jnp.concatenate([jnp.where(wide_low, tile, 0.0), jnp.where(wide_low, 0.0, tile)], axis=0).astype(BF16)
        push = dot_nn(lhs, leaf_transfer[2 * pair:2 * pair + 2].reshape(2 * r, child * r0)).astype(BF16)
        for s in range(2):
            for h in range(child // 4):
                q = (2 * pair + s) * (child // 4) + h
                b = jnp.concatenate([basis[:, q * 4 * m:(q + 1) * 4 * m]] * 4, axis=0) * quad_mask
                masked_basis[q] = b
                lhs = push[s * r:(s + 1) * r, h * 4 * r0:(h + 1) * 4 * r0]
                response[:, q * 4 * m:(q + 1) * 4 * m] = dot_nn(lhs, b).astype(BF16)

    for copy in index_copies:
        copy.wait()
    halo_arrive(1)
    spread_leaves(0)
    spread_leaves(2)
    loads[5].wait()

    def far_step(c, carry):
        parts = []
        for l in range(child):
            tiles = []
            for t in range(k0 // fold):
                piece = take(leaf_tiles, far_source[t * fold, c * child + l])
                for w in range(1, fold):
                    piece = jnp.where(lane_block == w, take(leaf_tiles, far_source[t * fold + w, c * child + l]), piece)
                tiles.append(piece)
            parts.append(jnp.concatenate(tiles, axis=1))
        lhs = jnp.concatenate(parts, axis=0).astype(BF16)
        matrix = far_coupling[c * child:(c + 1) * child].reshape(child * r0, k0 * r0)
        leaf_far[c] = diagonal(dot_nt(lhs, matrix), v, r0)
        return carry


    halo_arrive(0)
    halo_arrive(2)
    spread_pairs(mw, mid_tiles, groups, 0)
    spread_pairs(mw, mid_tiles, groups, 2)
    loads[4].wait()
    for g in range(groups // quad):
        parts = []
        for c in range(g * quad, (g + 1) * quad):
            tiles = []
            for t in range(k1 // 2):
                a = take(mid_tiles, mid_source[c, 2 * t])
                b = take(mid_tiles, mid_source[c, 2 * t + 1])
                tiles.append(jnp.where(half, a, b))
            parts.append(jnp.concatenate(tiles, axis=1))
        lhs = jnp.concatenate(parts, axis=0).astype(BF16)
        matrix = mid_coupling[g * quad:(g + 1) * quad].reshape(quad * r, k1 * r)
        mid_far[:, g * quad * r:(g + 1) * quad * r] = diagonal(dot_nt(lhs, matrix), v, r)

    def base_step(pair):
        tile = mid_far[:, pair * LANES:(pair + 1) * LANES]
        lhs = jnp.concatenate([jnp.where(low_lane, tile, 0.0), jnp.where(low_lane, 0.0, tile)], axis=0).astype(BF16)
        push = dot_nn(lhs, leaf_transfer[2 * pair:2 * pair + 2].reshape(2 * r, child * r0))
        for s in range(2):
            c = 2 * pair + s
            lhs = (leaf_far[c] + push[s * v:(s + 1) * v]).astype(BF16)
            for h in range(child // 4):
                q = c * (child // 4) + h
                base[:, q * 4 * m:(q + 1) * 4 * m] = dot_nn(lhs[:, h * 4 * r0:(h + 1) * 4 * r0], masked_basis[q])

    spread_pairs(cw, charge_tiles, leaves, 0)
    spread_pairs(cw, charge_tiles, leaves, 2)

    zero = jnp.zeros((2 * v, LANES), F32)

    def gather(first):
        pieces = []
        for i in range(4):
            slot = first + i
            x = take(charge_tiles, near_source[slot // LANES, slot % LANES])
            pieces.append(jnp.where(half, x, 0.0) if i % 2 == 0 else jnp.where(half, 0.0, x))
        upper = jnp.concatenate([pieces[0], pieces[1]], axis=0)
        lower = jnp.concatenate([pieces[2], pieces[3]], axis=0)
        return jnp.concatenate(
            [jnp.concatenate([upper, zero], axis=1), jnp.concatenate([zero, lower], axis=1)], axis=0).astype(BF16)

    def collect(b, u):
        c = contribution[pl.ds(b * 2 * LANES * v + u, 2 * LANES, stride=v), :]
        return dot_nn(assigned[b], c.astype(BF16))

    steps = side // 4
    spans = side // (2 * LANES)
    per_span = steps // spans
    every = per_span // v
    wide_half = lanes((leaves, LANES)) < m
    mixed_half = lanes((4 * v, LANES)) < m
    for g in range(steps):
        if g == PASS_AT * steps // 8:
            pass_on()
        if g % (steps // CHUNKS) == 0:
            near_load(g // (steps // CHUNKS), 0).wait()
            near_load(g // (steps // CHUNKS), 1).wait()
        lhs = jnp.concatenate([gather(g * 4), gather(side + g * 4)], axis=0)
        block = jnp.concatenate([
            near_blocks[:, g * 4 * m:(g + 1) * 4 * m],
            near_blocks[:, (side + g * 4) * m:(side + (g + 1) * 4) * m]], axis=0)
        out = dot_nt(lhs, block)
        contribution[g * 4 * v:(g + 1) * 4 * v, :] = jnp.where(mixed_half, out[:4 * v], out[4 * v:])
        if g * groups % steps == 0:
            c = g * groups // steps
            far_step(c, 0)
            if c % 2 == 1:
                base_step(c // 2)
        span = g // per_span
        if span > 0 and g % every == every - 1:
            u = g % per_span // every
            part = collect(span - 1, u)
            near_part[u] = part if span == 1 else near_part[u] + part

    for u in range(v):
        total = collect(spans - 1, u)
        if spans > 1:
            total = total + near_part[u]
        mixed = jnp.where(wide_half, total[:leaves], total[leaves:])
        near_rows[u * leaves:(u + 1) * leaves, :] = mixed + pltpu.roll(mixed, LANES // 2, 1)

    for q in range(leaves // 4):
        for w in range(2):
            leaf = q * 4 + 2 * w
            even = near_rows[pl.ds(leaf, v, stride=leaves), :]
            odd = near_rows[pl.ds(leaf + 1, v, stride=leaves), :]
            base[:, leaf * m:(leaf + 2) * m] += jnp.where(half, even, odd)

    take_all(all_recv, 1)

    def box(b):
        return gathered[b % in_layer * across_layers + b // in_layer]

    low_half = low_lane[:v // 2]
    lhs = []
    for tile in range(n // 2):
        a = box(2 * tile)
        b = box(2 * tile + 1)
        lhs.append(jnp.concatenate([
            jnp.where(low_half, a, pltpu.roll(b, LANES // 2, 1)),
            jnp.where(low_half, pltpu.roll(a, LANES // 2, 1), b)], axis=0))
    lhs = jnp.concatenate(lhs, axis=1).astype(BF16)
    downward = dot_nt(lhs, jnp.concatenate([weights[tile] for tile in range(n // 2)], axis=1)).astype(BF16)
    for q in range(leaves // 4):
        span = slice(q * 4 * m, (q + 1) * 4 * m)
        out_ref[:, span] = (base[:, span] + dot_nn(downward, response[:, span])).astype(BF16)

    take_all(all_send, 0)
    take_all(all_send, 1)
    for kind in range(3):
        halo_sent(kind)


def body(
    charges, leaf_basis, leaf_transfer, mid_transfer, far_source, far_coupling, mid_source, mid_coupling,
    box_coupling, top_transfer, top_coupling, near_target, near_source, near_count, near_blocks,
):
    n = lax.axis_size(AXIS)
    v, points = charges.shape
    leaves, k0 = far_source.shape
    m = points // leaves
    r0 = leaf_basis.shape[0]
    groups, k1 = mid_source.shape
    r = leaf_transfer.shape[1]
    capacity = near_target.shape[0]
    levels = (n // 4).bit_length() - 1
    tiles = sum((n >> level) // 2 + 1 for level in range(levels + 1))
    sizes = (v, leaves, m, r0, groups, r, k0, k1, capacity)
    vmem = pl.BlockSpec(memory_space=pltpu.VMEM)
    hbm = pl.BlockSpec(memory_space=pltpu.HBM)
    dma = pltpu.SemaphoreType.DMA
    return pl.pallas_call(
        functools.partial(kernel, n, sizes),
        out_shape=pltpu.VMEM(charges.shape, BF16),
        in_specs=[hbm] * 3 + [pl.BlockSpec(memory_space=pl.ANY)] + [hbm] * 11,
        out_specs=vmem,
        scratch_shapes=[
            pltpu.VMEM((3, v, points), BF16),
            pltpu.VMEM((3, v, leaves * r0), BF16),
            pltpu.VMEM((3, v, groups * r), BF16),
            pltpu.VMEM((n, v // 2, 2 * r), F32),
            pltpu.VMEM(leaf_basis.shape, BF16),
            pltpu.VMEM(leaf_transfer.shape, BF16),
            pltpu.VMEM(mid_transfer.shape[1:], BF16),
            pltpu.VMEM(far_coupling.shape, BF16),
            pltpu.VMEM(mid_coupling.shape, BF16),
            pltpu.VMEM(box_coupling.shape[1:], BF16),
            pltpu.VMEM(top_transfer.shape, BF16),
            pltpu.VMEM((levels,) + top_coupling.shape[1:], BF16),
            pltpu.VMEM(near_blocks.shape, BF16),
            pltpu.VMEM((capacity // LANES, LANES), jnp.int32),
            pltpu.VMEM((k0, leaves), jnp.int32),
            pltpu.VMEM((groups, k1), jnp.int32),
            pltpu.VMEM((capacity // LANES, LANES), jnp.int32),
            pltpu.SMEM((capacity // LANES, LANES), jnp.int32),
            pltpu.SMEM((k0, leaves), jnp.int32),
            pltpu.SMEM((groups, k1), jnp.int32),
            pltpu.VMEM((1, 1), jnp.int32),
            pltpu.VMEM((4 * leaves, v, LANES), F32),
            pltpu.VMEM((4 * leaves, v, LANES), F32),
            pltpu.VMEM((4 * groups, v, LANES), F32),
            pltpu.VMEM((capacity // 2 * v, 2 * m), F32),
            pltpu.VMEM((v, 2 * leaves, 2 * m), F32),
            pltpu.VMEM((v * leaves, 2 * m), F32),
            pltpu.VMEM((groups, v, leaves // groups * r0), F32),
            pltpu.VMEM((v, groups * r), F32),
            pltpu.VMEM((tiles, r, 2 * r), BF16),
            pltpu.VMEM((r, points), BF16),
            pltpu.VMEM((v, points), F32),
            pltpu.VMEM((leaves // 4, 4 * r0, 4 * m), BF16),
            pltpu.VMEM((capacity // LANES // 4, 2 * leaves, 2 * LANES), BF16),
            dma((13,)),
            dma((2 * CHUNKS,)),
            dma((levels,)),
            dma((3,)),
            dma((6,)),
            dma((6,)),
            dma((2,)),
            dma((2,)),
        ],
        compiler_params=pltpu.CompilerParams(
            collective_id=0, has_side_effects=True, vmem_limit_bytes=60 * 1024 * 1024),
    )(
        near_source.reshape(capacity // LANES, LANES), far_source.T, mid_source, near_count.reshape(1, 1), near_target.reshape(capacity // LANES, LANES),
        charges, leaf_basis, leaf_transfer, mid_transfer, far_coupling, mid_coupling,
        box_coupling, top_transfer, top_coupling, near_blocks,
    )


def solution(mesh):
    c = "clusters"
    in_specs = (
        P(None, c), P(None, c), P(c, None, None), P(c, None, None), P(c, None), P(c, None, None),
        P(c, None), P(c, None, None), P(c, None, None), P(), P(), P(c), P(c), P(c), P(None, c),
    )
    return jax.shard_map(body, mesh=mesh, in_specs=in_specs, out_specs=P(None, c), check_vma=False)
```
